256 devices in a mesh: node: 32 (over x, z_lo, core), local: 8 (over z_hi, y).
Axes of the slice: x: 4, y: 4, z: 8 (z_hi: 2, z_lo: 4; z = z_hi * 4 + z_lo), core: 2. Of those that a mesh axis runs over, the one named last changes fastest.
Arguments:
- grad_values: bfloat16 [256, 8192, 512], P(('node', 'local')), may hold values from -4 to 4
- grad_exponents: int32 [256, 4, 8192], P(('node', 'local')), may hold values from -1 to 2
- proj: float32 [8192, 256], P(('local', 'node')), may hold values from -1.5 to 1.5
- weights: float32 [8192, 512], P(('local', 'node')), may hold values from -4 to 4
- moment1: float32 [256, 512], P('node'), may hold values from -6 to 6
- moment2: float32 [256, 512], P('node'), may hold values from 1 to 100
Outputs:
- quant_values: bfloat16 [8192, 512], P('local')
- quant_scales: bfloat16 [4, 8192], P(None, 'local')
- new_weights: float32 [8192, 512], P(('local', 'node'))
- new_moment1: float32 [256, 512], P('node')
- new_moment2: float32 [256, 512], P('node')
The draws below stay inside these ranges and needn't reach their ends.
All inputs are finite; a program needn't handle non-finite values. Where the reference program divides by a largest or mean magnitude, that divisor is 1e-20 or more.
Results may differ from the reference program's by a relative error of at most 0.0085.
Values may be sent and summed in bfloat16 or wider, within the bound.
A program may use at most 128 MiB of HBM per device.

```python
import math
import jax
import jax.numpy as jnp
from jax import lax

D = 8192
COLS = 512
RANK = 256
BLOCK = 128
CB = 4
N_NODE = 32
N_LOCAL = 8


def set_ends(array, stream_key, smallest, high):
    shape = array.shape
    place = [jax.random.randint(jax.random.fold_in(stream_key, axis), (), 0, shape[axis]) for axis in range(len(shape))]
    array = array.at[tuple(place)].set(smallest)
    longest = shape.index(max(shape))
    place[longest] = (place[longest] + 1) % shape[longest]
    return array.at[tuple(place)].set(high)


def strengthened(drawn, rng, source, target, shards_of, factor):
    owner, partner = [(jnp.arange(drawn.shape[axis_at]) // (drawn.shape[axis_at] // shards_of)).reshape([-1 if axis == axis_at else 1 for axis in range(drawn.ndim)]) for axis_at in (source, target)]
    chosen = jax.random.permutation(rng, shards_of)[partner]
    strong = (owner == chosen) | (owner == (partner + shards_of // 2) % shards_of)
    return jnp.where(strong, factor * drawn, drawn)


def steps_of(key, shape, cuts, least, largest):
    def one(position, parts):
        heights = jax.random.uniform(jax.random.fold_in(jax.random.fold_in(key, 6), position), (parts,), jnp.float32, least / len(cuts), largest / len(cuts))
        return jnp.repeat(jnp.exp(heights), shape[position] // parts).reshape((-1,) + (1,) * (len(shape) - position - 1))

    loudness = one(*cuts[0])
    for cut in cuts[1:]:
        loudness = loudness * one(*cut)
    return loudness


def normal_values(own_key, dims, deviation, bound, pieces=(), held_as=jnp.bfloat16):
    drawn = jax.random.normal(own_key, dims, jnp.float32) * deviation
    if len(pieces) > 0:
        drawn = steps_of(own_key, dims, pieces, -0.22, 0.18) * drawn
    return jnp.clip(drawn, min=-bound, max=bound).astype(held_as)


def noise_with(own_key, dims, scale, most, pieces, heavy, held_as=jnp.bfloat16):
    entries = scale * jax.random.normal(own_key, dims, jnp.float32)
    if pieces:
        entries = entries * steps_of(own_key, dims, pieces, -0.22, 0.18)
    return jnp.clip(strengthened(entries, jax.random.fold_in(own_key, 3), *heavy), -most, most).astype(held_as)


def setup_inputs(seed: int = 0) -> dict:
    key_of = jax.random.split(jax.random.key(seed), 7)
    grad_values = noise_with(key_of[0], (N_NODE * N_LOCAL, D, COLS), 0.0625, 4.0, ((0, 256),), (0, 1, 256, 6.0))
    grad_exponents = set_ends(jax.random.randint(key_of[1], (N_NODE * N_LOCAL, CB, D), -1, 3), jax.random.fold_in(key_of[1], 1), -1, 2).astype(jnp.int32)
    proj = noise_with(key_of[2], (D, RANK), RANK ** -0.5, 1.5, ((0, 256),), (0, 1, 256, 6.0), jnp.float32)
    weights = normal_values(key_of[3], (D, COLS), 0.25, 4.0, ((0, 256),), jnp.float32)
    moment1 = normal_values(key_of[4], (RANK, COLS), 1.0, 6.0, ((0, 32),), jnp.float32)
    moment2 = jnp.clip(jnp.exp(math.log(100.0) - 4.6051702 * jax.random.uniform(key_of[5], (RANK, COLS), jnp.float32) ** steps_of(key_of[5], (RANK, COLS), ((0, 32),), -0.2, 0.2)), 1.0, 100.0)
    return dict(grad_values=grad_values, grad_exponents=grad_exponents, proj=proj, weights=weights, moment1=moment1, moment2=moment2)


bias_first = 1.0 - 0.9 ** 10
bias_second = 1.0 - 0.999 ** 10

def reference(grad_values, grad_exponents, proj, weights, moment1, moment2):

    def add_partial(index, total):
        mantissa = grad_values[index].astype(jnp.float32)
        factor = jnp.exp2(grad_exponents[index].astype(jnp.float32))
        scaled = mantissa.reshape(D, CB, BLOCK) * jnp.transpose(factor)[:, :, None]
        return total + scaled.reshape(D, COLS)
    grad = lax.fori_loop(0, N_NODE * N_LOCAL, add_partial, jnp.zeros((D, COLS), jnp.float32))
    projected = jnp.dot(jnp.transpose(proj), grad, precision=lax.Precision.HIGHEST, preferred_element_type=jnp.float32)
    new_moment1 = 0.9 * moment1 + 0.1 * projected
    new_moment2 = 0.999 * moment2 + 0.001 * projected * projected
    tilde = new_moment1 / bias_first / (jnp.sqrt(new_moment2 / bias_second) + 1e-08)
    col_scale = jnp.sqrt(lax.optimization_barrier(jnp.sum(tilde * tilde, 0))) / jnp.sqrt(lax.optimization_barrier(jnp.sum(projected * projected, 0)) + 1e-06)
    new_weights = weights - 8.0 * grad * col_scale[None, :]
    blocks = new_weights.reshape(D, CB, BLOCK)
    block_max = (lax.optimization_barrier(jnp.max(jnp.abs(blocks), 2)) + 1e-06).astype(jnp.bfloat16)
    quant_values = (blocks / block_max.astype(jnp.float32)[:, :, None]).reshape(D, COLS).astype(jnp.bfloat16)
    quant_scales = jnp.transpose(block_max)
    return (quant_values, quant_scales, new_weights, new_moment1, new_moment2)
```

```python
import functools

import jax
import jax.numpy as jnp
from jax import lax
from jax.experimental import pallas as pl
from jax.experimental.pallas import tpu as pltpu
from jax.sharding import PartitionSpec as P

MESH = pl.DeviceIdType.MESH
BIAS1 = 1.0 - 0.9**10
BIAS2 = 1.0 - 0.999**10
F32 = jnp.float32
BF16 = jnp.bfloat16
NCOPY = 160


def kernel(
    gv, ex, proj, wts, mom1, mom2,
    o_qv, o_qs, o_nw, o_m1, o_m2,
    M0, M1, S, RA, RB, S2, RA2, RB2, G2, RG, PA, PT, PP, RP, TQ, RQ, AZ, RZ,
    MO, VS, VX, W32, WG, GG, G32, E0, E1, MI, QV, QS, NW, ONE,
    ss, rs, ls,
):
    node = lax.axis_index("node")
    local = lax.axis_index("local")
    x = lax.div(node, 8)
    zl = lax.rem(lax.div(node, 2), 4)
    c = lax.rem(node, 2)
    zh = lax.div(local, 4)
    y = lax.rem(local, 4)
    z = zh * 4 + zl
    oc = 1 - c

    def dev(dx=0, dy=0, dz=0, core=None, dzl=None):
        xx = lax.rem(x + dx, 4)
        yy = lax.rem(y + dy, 4)
        if dzl is None:
            zz = lax.rem(z + dz, 8)
        else:
            zz = zh * 4 + lax.rem(zl + dzl, 4)
        cc = c if core is None else core
        return (xx * 8 + lax.rem(zz, 4) * 2 + cc, lax.div(zz, 4) * 4 + yy)

    counter = [0]
    copies = []

    def remote(src, dst, to):
        i = counter[0]
        counter[0] += 1
        r = pltpu.make_async_remote_copy(
            src_ref=src, dst_ref=dst, send_sem=ss.at[i], recv_sem=rs.at[i],
            device_id=to, device_id_type=MESH)
        r.start()
        copies.append(r)
        return r

    lcount = [0]

    def localcopy(src, dst):
        i = lcount[0]
        lcount[0] += 1
        r = pltpu.make_async_copy(src, dst, ls.at[i])
        r.start()
        return r

    partners = [dev(core=oc)]
    partners += [dev(dx=i, dy=j) for i in range(4) for j in range(4) if (i, j) != (0, 0)]
    partners += [dev(dz=k) for k in range(1, 8)]
    partners += [dev(dzl=k, core=oc) for k in range(1, 4)]
    barrier = pltpu.get_barrier_semaphore()
    for d in partners:
        pl.semaphore_signal(barrier, inc=1, device_id=d, device_id_type=MESH)

    REL = (2, 1, 3, 0)
    ORDER = ((0, 0), (0, 1), (1, 1), (2, 0), (1, 0), (2, 1), (3, 0), (3, 1))

    def dest(k, di):
        return lax.rem((x if k == 0 else y) + REL[di], 4)

    def gslice(k, di, h, core):
        d = dest(k, di)
        rows = pl.ds(16 * k, 16)
        if k == 0:
            return gv.at[pl.ds(h * 4, 4), d, :, core, rows, :]
        return gv.at[h * 4 + d, :, :, core, rows, :]

    ld_e = localcopy(ex, E0)
    loads = {}
    for di, h in ORDER:
        for k in range(2):
            loads[k, di, h] = localcopy(gslice(k, di, h, c), M0.at[k, di, h])
    ld_w = localcopy(wts, W32)
    ld_p = localcopy(proj, PA.at[z])
    ld_m = [localcopy(mom1, MI.at[0]), localcopy(mom2, MI.at[1])]
    ONE[...] = jnp.ones((128, 128), BF16)

    pl.semaphore_wait(barrier, len(partners))

    sendE = remote(ex, E1, dev(core=oc))
    sends = {}
    for di, h in ORDER:
        for k in range(2):
            sends[k, di, h] = remote(gslice(k, di, h, oc), M1.at[k, di, h], dev(core=oc))
    pas = [remote(proj, PA.at[z], dev(dz=k)) for k in range(1, 8)]

    ld_w.wait()
    WG[x, zl, c] = W32[...].astype(BF16)

    lane = lax.broadcasted_iota(jnp.int32, (32, 128), 1)
    row = lax.broadcasted_iota(jnp.int32, (32, 128), 0)
    hit0 = row + jnp.where(row >= 16, 48, 0) + c * 32
    masks = [lane == hit0, lane == hit0 + 16]

    def dequant(k, di, h):
        d = dest(k, di)

        def body(q, carry):
            for t in range(2):
                base = (((h * 4 + q) * 4 + d) if k == 0 else ((h * 4 + d) * 4 + q)) * 256 + t * 128
                base = pl.multiple_of(base, 128)
                facs = []
                for E in (E0, E1):
                    e = E[:, pl.ds(base, 128)]
                    f = 0.5 * lax.shift_left(jnp.ones_like(e), e + 1).astype(F32)
                    lhs = jnp.concatenate(
                        [jnp.where(masks[k], f[b:b + 1, :], 0.0) for b in range(4)], 0
                    ).astype(BF16)
                    facs.append(jnp.dot(lhs, ONE[...], preferred_element_type=F32))
                for zz in range(2):
                    for b in range(4):
                        cols = pl.ds(b * 128, 128)
                        r0 = (b * 2 + zz) * 16
                        v = (
                            M0[k, di, h, q, 2 * t + zz, :, cols].astype(F32) * facs[0][r0:r0 + 16]
                            + M1[k, di, h, q, 2 * t + zz, :, cols].astype(F32) * facs[1][r0:r0 + 16]
                        )
                        S[k, di, h, q, 2 * t + zz, :, cols] = v.astype(BF16)
            return carry

        lax.fori_loop(0, 4, body, 0, unroll=2)

    def nb(k, stage, step):
        if (k + stage) % 2 == 0:
            return dev(dx=step)
        return dev(dy=step)

    ld_e.wait()
    sendE.wait_recv()
    RAc, RBc = {}, {}

    def addinto(dst, src):
        def body(i, carry):
            q, r = lax.div(i, 4), lax.rem(i, 4)
            dst[q, r] = (dst[q, r].astype(F32) + src[q, r].astype(F32)).astype(BF16)
            return carry
        lax.fori_loop(0, 16, body, 0, unroll=4)

    wx = None
    for n, (di, h) in enumerate(ORDER):
        for k in range(2):
            loads[k, di, h].wait()
            sends[k, di, h].wait_recv()
            dequant(k, di, h)
            step = 1 if h == 0 else 3
            if di == 0:
                RAc[k, h] = remote(S.at[k, 0, h], RA.at[k, h], nb(k, 0, step))
            elif (di, h) == (1, 1):
                RBc[k, 0, 1] = remote(S.at[k, 1, 1], RB.at[k, 0, 1], nb(k, 0, 1))
            elif (di, h) == (2, 0):
                RBc[k, 1, 0] = remote(S.at[k, 2, 0], RB.at[k, 1, 0], nb(k, 0, 3))
        if n == 3:
            wx = [remote(WG.at[x, zl, c], WG.at[x, zl, c], dev(dx=i)) for i in range(1, 4)]
    for h in range(2):
        for k in range(2):
            RAc[k, h].wait_recv()
            di = 1 if h == 0 else 2
            addinto(S.at[k, di, h], RA.at[k, h])
            if h == 0:
                RBc[k, 0, 0] = remote(S.at[k, 1, 0], RB.at[k, 0, 0], nb(k, 0, 1))
            else:
                RBc[k, 1, 1] = remote(S.at[k, 2, 1], RB.at[k, 1, 1], nb(k, 0, 3))

    for r in wx:
        r.wait_recv()
    wz = [remote(WG.at[:, zl, c], WG.at[:, zl, c], dev(dzl=i)) for i in range(1, 4)]

    ld_p.wait()
    for r in pas:
        r.wait_recv()
    pt = jnp.transpose(PA[...].reshape(256, 256))
    hi = pt.astype(BF16)
    rest = pt - hi.astype(F32)
    mid = rest.astype(BF16)
    PT[0] = hi
    PT[1] = mid
    PT[2] = (rest - mid.astype(F32)).astype(BF16)

    RAc2, RBc2 = {}, {}

    def finish1(k, di, h):
        a = lax.rem((y if k == 0 else x) + REL[di], 4)
        for r in range(4):
            v = (S[k, 3, h, a, r].astype(F32) + RB[k, 0, h, a, r].astype(F32)
                 + RB[k, 1, h, a, r].astype(F32))
            S2[k, di, h, r] = v.astype(BF16)

    for k in range(2):
        for s in range(2):
            for h in ((1, 0) if s == 0 else (0, 1)):
                RBc[k, s, h].wait_recv()
    for di, h in ORDER:
        for k in range(2):
            finish1(k, di, h)
            step = 1 if h == 0 else 3
            if di == 0:
                RAc2[k, h] = remote(S2.at[k, 0, h], RA2.at[k, h], nb(k, 1, step))
            elif (di, h) == (1, 1):
                RBc2[k, 0, 1] = remote(S2.at[k, 1, 1], RB2.at[k, 0, 1], nb(k, 1, 1))
            elif (di, h) == (2, 0):
                RBc2[k, 1, 0] = remote(S2.at[k, 2, 0], RB2.at[k, 1, 0], nb(k, 1, 3))
    for h in range(2):
        for k in range(2):
            RAc2[k, h].wait_recv()
            di = 1 if h == 0 else 2
            for r in range(4):
                S2[k, di, h, r] = (S2[k, di, h, r].astype(F32) + RA2[k, h, r].astype(F32)).astype(BF16)
            if h == 0:
                RBc2[k, 0, 0] = remote(S2.at[k, 1, 0], RB2.at[k, 0, 0], nb(k, 1, 1))
            else:
                RBc2[k, 1, 1] = remote(S2.at[k, 2, 1], RB2.at[k, 1, 1], nb(k, 1, 3))
    for k in range(2):
        for s in range(2):
            for h in ((1, 0) if s == 0 else (0, 1)):
                RBc2[k, s, h].wait_recv()
        for h in range(2):
            for r in range(4):
                v = (S2[k, 3, h, r].astype(F32) + RB2[k, 0, h, r].astype(F32)
                     + RB2[k, 1, h, r].astype(F32))
                G2[h * 4 + r, pl.ds(16 * k, 16), :] = v.astype(BF16)

    gz = [remote(G2.at[lax.rem(z + k, 8)], RG.at[z], dev(dz=k)) for k in (4, 3, 5, 2, 6, 1, 7)]

    g2 = G2[...].reshape(256, 512)
    part = (jnp.dot(PT[0], g2, preferred_element_type=F32)
            + jnp.dot(PT[1], g2, preferred_element_type=F32)
            + jnp.dot(PT[2], g2, preferred_element_type=F32))
    PP[...] = part.reshape(4, 4, 2, 8, 512)
    pc = remote(PP.at[:, :, oc], RP, dev(core=oc))
    pc.wait_recv()
    for i in range(4):
        for r in range(4):
            v = PP[i, r, c] + RP[i, r]
            for j in range(4):
                TQ[i, j, r] = v[:, j * 128:(j + 1) * 128]
    RQ[x, y] = TQ[x, y]
    qs = [remote(TQ.at[lax.rem(x + i, 4), lax.rem(y + j, 4)], RQ.at[x, y], dev(dx=i, dy=j))
          for i in range(4) for j in range(4) if (i, j) != (0, 0)]
    for r in qs:
        r.wait_recv()
    acc = RQ[0, 0]
    for i in range(1, 16):
        acc = acc + RQ[i // 4, i % 4]
    AZ[...] = acc
    RZ[z] = AZ[zl]
    zs = [remote(AZ.at[lax.rem(zl + k, 4)], RZ.at[z], dev(dz=k)) for k in range(1, 8)]

    for r in wz:
        r.wait_recv()
    wc = remote(WG.at[:, :, c], WG.at[:, :, c], dev(core=oc))

    for r in gz:
        r.wait_recv()
    RG[z] = G2[z]
    g = RG[0].astype(F32)
    for i in range(1, 8):
        g = g + RG[i].astype(F32)
    G32[...] = g
    GG[x, zl, c] = g.astype(BF16)
    ga = [remote(GG.at[x, zl, c], GG.at[x, zl, c], dev(dzl=i)) for i in range(1, 4)]

    for r in zs:
        r.wait_recv()
    pj = RZ[0]
    for i in range(1, 8):
        pj = pj + RZ[i]
    for r in ld_m:
        r.wait()
    ycol = pl.ds(pl.multiple_of(y * 128, 128), 128)
    first = 0.9 * MI[0, :, ycol] + 0.1 * pj
    second = 0.999 * MI[1, :, ycol] + 0.001 * pj * pj
    tilde = first / BIAS1 / (jnp.sqrt(second / BIAS2) + 1e-08)
    raw = jnp.sum(pj * pj, 0, keepdims=True)
    til = jnp.sum(tilde * tilde, 0, keepdims=True)
    r8 = lax.broadcasted_iota(jnp.int32, (8, 128), 0)
    VS[zl, c] = jnp.where(r8 == 0, raw, jnp.where(r8 == 1, til, 0.0))
    vs = [remote(VS.at[zl, c], VS.at[zl, c], dev(dzl=i, core=cc))
          for i, cc in ((2, c), (2, oc), (1, c), (3, c), (1, oc), (3, oc), (0, oc))]
    MO[y, 0] = first
    MO[y, 1] = second
    mo = [remote(MO.at[y], MO.at[y], dev(dy=i)) for i in range(1, 4)]
    for r in vs:
        r.wait_recv()
    v = VS[0, 0]
    for i in range(1, 8):
        v = v + VS[i // 2, i % 2]
    VX[x, y] = v
    vx = [remote(VX.at[x, y], VX.at[x, y], dev(dx=i, dy=j))
          for i, j in ((2, 2), (1, 2), (3, 2), (2, 1), (2, 3), (0, 2), (2, 0), (1, 1), (1, 3), (3, 1),
                       (3, 3), (0, 1), (0, 3), (1, 0), (3, 0))]
    for r in ga:
        r.wait_recv()
    gx = [remote(GG.at[x, :, c], GG.at[x, :, c], dev(dx=i)) for i in (2, 1, 3)]
    outs = []
    for r in mo:
        r.wait_recv()
    for j in range(4):
        outs.append(localcopy(MO.at[j, 0], o_m1.at[:, pl.ds(128 * j, 128)]))
        outs.append(localcopy(MO.at[j, 1], o_m2.at[:, pl.ds(128 * j, 128)]))
    for r in vx:
        r.wait_recv()
    cs = []
    for j in range(4):
        t = VX[0, j] + VX[1, j] + VX[2, j] + VX[3, j]
        cs.append(8.0 * (jnp.sqrt(t[1:2]) / jnp.sqrt(t[0:1] + 1e-06)))
    for j in range(4):
        cols = pl.ds(128 * j, 128)
        NW[:, cols] = W32[:, cols] - G32[:, cols] * cs[j]
    outs.append(localcopy(NW, o_nw))
    for r in gx:
        r.wait_recv()
    gc = remote(GG.at[:, :, c], GG.at[:, :, c], dev(core=oc))
    wc.wait_recv()
    gc.wait_recv()

    eye = (lax.broadcasted_iota(jnp.int32, (8, 128), 0)
           == lax.broadcasted_iota(jnp.int32, (8, 128), 1)).astype(BF16)
    lane32 = lax.broadcasted_iota(jnp.int32, (32, 128), 1)

    def quant(i, carry):
        stack = []
        for u in range(4):
            n = i * 4 + u
            nx, nz, nc = lax.div(n, 8), lax.rem(lax.div(n, 2), 4), u % 2
            packed = jnp.zeros((32, 128), F32)
            for j in range(4):
                cols = pl.ds(128 * j, 128)
                v = WG[nx, nz, nc, :, cols].astype(F32) - GG[nx, nz, nc, :, cols].astype(F32) * cs[j]
                scale = (jnp.max(jnp.abs(v), 1, keepdims=True) + 1e-06).astype(BF16).astype(F32)
                QV[pl.ds(pl.multiple_of(n * 32, 32), 32), cols] = (v / scale).astype(BF16)
                packed = jnp.where(lane32 == j, scale, packed)
            stack.append(packed.astype(BF16))
        st = jnp.concatenate(stack, 0)
        tr = lax.dot_general(eye, st, (((1,), (1,)), ((), ())), preferred_element_type=F32)
        QS[:, pl.ds(pl.multiple_of(i * 128, 128), 128)] = tr[:4].astype(BF16)
        return carry

    lax.fori_loop(0, 8, quant, 0)
    outs.append(localcopy(QV, o_qv))
    outs.append(localcopy(QS, o_qs))
    for r in outs:
        r.wait()
    for r in copies:
        r.wait_send()


def shards(grad_values, grad_exponents, proj, weights, moment1, moment2):
    gv = grad_values.reshape(8, 4, 4, 2, 32, 512)
    ex = grad_exponents.reshape(4, 8192)
    any_ = pl.BlockSpec(memory_space=pl.ANY)
    V = pltpu.VMEM
    scratch = [
        V((2, 4, 2, 4, 4, 16, 512), BF16),
        V((2, 4, 2, 4, 4, 16, 512), BF16),
        V((2, 4, 2, 4, 4, 16, 512), BF16),
        V((2, 2, 4, 4, 16, 512), BF16),
        V((2, 2, 2, 4, 4, 16, 512), BF16),
        V((2, 4, 2, 4, 16, 512), BF16),
        V((2, 2, 4, 16, 512), BF16),
        V((2, 2, 2, 4, 16, 512), BF16),
        V((8, 32, 512), BF16),
        V((8, 32, 512), BF16),
        V((8, 32, 256), F32),
        V((3, 256, 256), BF16),
        V((4, 4, 2, 8, 512), F32),
        V((4, 4, 8, 512), F32),
        V((4, 4, 4, 8, 128), F32),
        V((4, 4, 4, 8, 128), F32),
        V((4, 8, 128), F32),
        V((8, 8, 128), F32),
        V((4, 2, 8, 128), F32),
        V((4, 2, 8, 128), F32),
        V((4, 4, 8, 128), F32),
        V((32, 512), F32),
        V((4, 4, 2, 32, 512), BF16),
        V((4, 4, 2, 32, 512), BF16),
        V((32, 512), F32),
        V((4, 8192), jnp.int32),
        V((4, 8192), jnp.int32),
        V((2, 8, 512), F32),
        V((1024, 512), BF16),
        V((4, 1024), BF16),
        V((32, 512), F32),
        V((128, 128), BF16),
        pltpu.SemaphoreType.DMA((NCOPY,)),
        pltpu.SemaphoreType.DMA((NCOPY,)),
        pltpu.SemaphoreType.DMA((40,)),
    ]
    return pl.pallas_call(
        kernel,
        out_shape=(
            jax.ShapeDtypeStruct((1024, 512), BF16),
            jax.ShapeDtypeStruct((4, 1024), BF16),
            jax.ShapeDtypeStruct((32, 512), F32),
            jax.ShapeDtypeStruct((8, 512), F32),
            jax.ShapeDtypeStruct((8, 512), F32),
        ),
        in_specs=[any_] * 6,
        out_specs=(any_,) * 5,
        scratch_shapes=scratch,
        compiler_params=pltpu.CompilerParams(
            collective_id=0, has_side_effects=True, vmem_limit_bytes=60 * 1024 * 1024
        ),
    )(gv, ex, proj, weights, moment1, moment2)


def solution(mesh):
    return jax.shard_map(
        shards,
        mesh=mesh,
        in_specs=(
            P(("node", "local"), None, None),
            P(("node", "local"), None, None),
            P(("local", "node"), None),
            P(("local", "node"), None),
            P("node", None),
            P("node", None),
        ),
        out_specs=(
            P("local", None),
            P(None, "local"),
            P(("local", "node"), None),
            P("node", None),
            P("node", None),
        ),
        check_vma=False,
    )
```

```python
import functools

import jax
import jax.numpy as jnp
from jax import lax
from jax.experimental import pallas as pl
from jax.experimental.pallas import tpu as pltpu
from jax.sharding import PartitionSpec as P

MESH = pl.DeviceIdType.MESH
BIAS1 = 1.0 - 0.9**10
BIAS2 = 1.0 - 0.999**10
F32 = jnp.float32
BF16 = jnp.bfloat16
NCOPY = 160
PRE = 10


def kernel(
    gv, ex, proj, wts, mom1, mom2,
    o_wg, o_gg, o_g, o_cs, o_mo,
    M0, M1, S, RA, RB, S2, RA2, RB2, G2, RG, PA, PT, PP, RP, TQ, RQ, AZ, RZ,
    MO, VS, VX, W32, WG, GG, G32, E0, E1, MI, CS, ONE,
    ss, rs, ls,
):
    node = lax.axis_index("node")
    local = lax.axis_index("local")
    x = lax.div(node, 8)
    zl = lax.rem(lax.div(node, 2), 4)
    c = lax.rem(node, 2)
    zh = lax.div(local, 4)
    y = lax.rem(local, 4)
    z = zh * 4 + zl
    oc = 1 - c

    def dev(dx=0, dy=0, dz=0, core=None, dzl=None):
        xx = lax.rem(x + dx, 4)
        yy = lax.rem(y + dy, 4)
        if dzl is None:
            zz = lax.rem(z + dz, 8)
        else:
            zz = zh * 4 + lax.rem(zl + dzl, 4)
        cc = c if core is None else core
        return (xx * 8 + lax.rem(zz, 4) * 2 + cc, lax.div(zz, 4) * 4 + yy)

    counter = [0]
    copies = []

    def remote(src, dst, to):
        i = counter[0]
        counter[0] += 1
        r = pltpu.make_async_remote_copy(
            src_ref=src, dst_ref=dst, send_sem=ss.at[i], recv_sem=rs.at[i],
            device_id=to, device_id_type=MESH)
        r.start()
        copies.append(r)
        return r

    lcount = [0]

    def localcopy(src, dst):
        i = lcount[0]
        lcount[0] += 1
        r = pltpu.make_async_copy(src, dst, ls.at[i])
        r.start()
        return r

    partners = [dev(core=oc)]
    partners += [dev(dx=i, dy=j) for i in range(4) for j in range(4) if (i, j) != (0, 0)]
    partners += [dev(dz=k) for k in range(1, 8)]
    partners += [dev(dzl=k, core=oc) for k in range(1, 4)]
    barrier = pltpu.get_barrier_semaphore()
    for d in partners:
        pl.semaphore_signal(barrier, inc=1, device_id=d, device_id_type=MESH)

    REL = (2, 1, 3, 0)
    ORDER = ((0, 0), (0, 1), (1, 1), (2, 0), (1, 0), (2, 1), (3, 0), (3, 1))

    def dest(k, di):
        return lax.rem((x if k == 0 else y) + REL[di], 4)

    def gslice(k, di, h, core):
        d = dest(k, di)
        rows = pl.ds(16 * k, 16)
        if k == 0:
            return gv.at[pl.ds(h * 4, 4), d, :, core, rows, :]
        return gv.at[h * 4 + d, :, :, core, rows, :]

    ld_e = localcopy(ex, E0)
    loads = {}
    for di, h in ORDER:
        for k in range(2):
            loads[k, di, h] = localcopy(gslice(k, di, h, c), M0.at[k, di, h])
    ld_w = localcopy(wts, W32)
    ld_p = localcopy(proj, PA.at[z])
    ld_m = [localcopy(mom1, MI.at[0]), localcopy(mom2, MI.at[1])]
    ONE[...] = jnp.ones((128, 128), BF16)

    lane = lax.broadcasted_iota(jnp.int32, (32, 128), 1)
    row = lax.broadcasted_iota(jnp.int32, (32, 128), 0)
    hit0 = row + jnp.where(row >= 16, 48, 0) + c * 32
    masks = [lane == hit0, lane == hit0 + 16]

    def factors(E, k, di, h, q):
        d = dest(k, di)
        rows = []
        for u in range(2):
            for t in range(2):
                base = (((h * 4 + q + u) * 4 + d) if k == 0 else ((h * 4 + d) * 4 + q + u)) * 256 + t * 128
                e = E[:, pl.ds(pl.multiple_of(base, 128), 128)]
                f = 0.5 * lax.shift_left(jnp.ones_like(e), e + 1).astype(F32)
                rows += [jnp.where(masks[k], f[b:b + 1, :], 0.0).astype(BF16) for b in range(4)]
        return jnp.dot(jnp.concatenate(rows, 0), ONE[...], preferred_element_type=F32).astype(BF16)

    def dequant(k, di, h, E, M, add):
        def body(p, carry):
            q = p * 2
            fac = factors(E, k, di, h, q)
            for u in range(2):
                for t in range(2):
                    for b in range(4):
                        for zz in range(2):
                            cols = pl.ds(b * 128, 128)
                            r0 = (((u * 2 + t) * 4 + b) * 2 + zz) * 16
                            v = M[k, di, h, q + u, 2 * t + zz, :, cols] * fac[r0:r0 + 16]
                            if add:
                                v = S[k, di, h, q + u, 2 * t + zz, :, cols] + v
                            S[k, di, h, q + u, 2 * t + zz, :, cols] = v
            return carry

        lax.fori_loop(0, 2, body, 0)

    ld_w.wait()
    WG[x, zl, c] = W32[...].astype(BF16)
    ld_e.wait()
    UNITS = [(k, di, h) for di, h in ORDER for k in range(2)]
    for n, (k, di, h) in enumerate(UNITS):
        if n == PRE:
            break
        loads[k, di, h].wait()
        dequant(k, di, h, E0, M0, False)

    pl.semaphore_wait(barrier, len(partners))

    sendE = remote(ex, E1, dev(core=oc))
    wx = [remote(WG.at[x, zl, c], WG.at[x, zl, c], dev(dx=i)) for i in range(1, 4)]
    sends = {}
    for di, h in ORDER:
        for k in range(2):
            sends[k, di, h] = remote(gslice(k, di, h, oc), M1.at[k, di, h], dev(core=oc))
    pas = [remote(proj, PA.at[z], dev(dz=k)) for k in range(1, 8)]

    def nb(k, stage, step):
        if (k + stage) % 2 == 0:
            return dev(dx=step)
        return dev(dy=step)

    for k, di, h in UNITS[PRE:]:
        loads[k, di, h].wait()
        dequant(k, di, h, E0, M0, False)
    sendE.wait_recv()
    RAc, RBc = {}, {}

    def addinto(dst, src):
        def body(i, carry):
            q, r = lax.div(i, 4), lax.rem(i, 4)
            dst[q, r] = dst[q, r] + src[q, r]
            return carry
        lax.fori_loop(0, 16, body, 0, unroll=4)

    for n, (di, h) in enumerate(ORDER):
        for k in range(2):
            sends[k, di, h].wait_recv()
            dequant(k, di, h, E1, M1, True)
            step = 1 if h == 0 else 3
            if di == 0:
                RAc[k, h] = remote(S.at[k, 0, h], RA.at[k, h], nb(k, 0, step))
            elif (di, h) == (1, 1):
                RBc[k, 0, 1] = remote(S.at[k, 1, 1], RB.at[k, 0, 1], nb(k, 0, 1))
            elif (di, h) == (2, 0):
                RBc[k, 1, 0] = remote(S.at[k, 2, 0], RB.at[k, 1, 0], nb(k, 0, 3))
        if n == 3:
            for r in wx:
                r.wait_recv()
            wz = [remote(WG.at[:, zl, c], WG.at[:, zl, c], dev(dzl=i)) for i in range(1, 4)]
    for h in range(2):
        for k in range(2):
            RAc[k, h].wait_recv()
            di = 1 if h == 0 else 2
            addinto(S.at[k, di, h], RA.at[k, h])
            if h == 0:
                RBc[k, 0, 0] = remote(S.at[k, 1, 0], RB.at[k, 0, 0], nb(k, 0, 1))
            else:
                RBc[k, 1, 1] = remote(S.at[k, 2, 1], RB.at[k, 1, 1], nb(k, 0, 3))


    ld_p.wait()
    for r in pas:
        r.wait_recv()
    pt = jnp.transpose(PA[...].reshape(256, 256))
    hi = pt.astype(BF16)
    rest = pt - hi.astype(F32)
    mid = rest.astype(BF16)
    PT[0] = hi
    PT[1] = mid
    PT[2] = (rest - mid.astype(F32)).astype(BF16)

    RAc2, RBc2 = {}, {}

    def finish1(k, di, h):
        a = lax.rem((y if k == 0 else x) + REL[di], 4)
        for r in range(4):
            v = (S[k, 3, h, a, r].astype(F32) + RB[k, 0, h, a, r].astype(F32)
                 + RB[k, 1, h, a, r].astype(F32))
            S2[k, di, h, r] = v.astype(BF16)

    for k in range(2):
        for s in range(2):
            for h in ((1, 0) if s == 0 else (0, 1)):
                RBc[k, s, h].wait_recv()
    for di, h in ORDER:
        for k in range(2):
            finish1(k, di, h)
            step = 1 if h == 0 else 3
            if di == 0:
                RAc2[k, h] = remote(S2.at[k, 0, h], RA2.at[k, h], nb(k, 1, step))
            elif (di, h) == (1, 1):
                RBc2[k, 0, 1] = remote(S2.at[k, 1, 1], RB2.at[k, 0, 1], nb(k, 1, 1))
            elif (di, h) == (2, 0):
                RBc2[k, 1, 0] = remote(S2.at[k, 2, 0], RB2.at[k, 1, 0], nb(k, 1, 3))
    for h in range(2):
        for k in range(2):
            RAc2[k, h].wait_recv()
            di = 1 if h == 0 else 2
            for r in range(4):
                S2[k, di, h, r] = S2[k, di, h, r] + RA2[k, h, r]
            if h == 0:
                RBc2[k, 0, 0] = remote(S2.at[k, 1, 0], RB2.at[k, 0, 0], nb(k, 1, 1))
            else:
                RBc2[k, 1, 1] = remote(S2.at[k, 2, 1], RB2.at[k, 1, 1], nb(k, 1, 3))
    for k in range(2):
        for s in range(2):
            for h in ((1, 0) if s == 0 else (0, 1)):
                RBc2[k, s, h].wait_recv()
        for h in range(2):
            for r in range(4):
                v = (S2[k, 3, h, r].astype(F32) + RB2[k, 0, h, r].astype(F32)
                     + RB2[k, 1, h, r].astype(F32))
                G2[h * 4 + r, pl.ds(16 * k, 16), :] = v.astype(BF16)

    gz = [remote(G2.at[lax.rem(z + k, 8)], RG.at[z], dev(dz=k)) for k in (4, 3, 5, 2, 6, 1, 7)]

    g2 = G2[...].reshape(256, 512)
    part = (jnp.dot(PT[0], g2, preferred_element_type=F32)
            + jnp.dot(PT[1], g2, preferred_element_type=F32)
            + jnp.dot(PT[2], g2, preferred_element_type=F32))
    PP[...] = part.reshape(4, 4, 2, 8, 512)
    pc = remote(PP.at[:, :, oc], RP, dev(core=oc))
    pc.wait_recv()
    for i in range(4):
        for r in range(4):
            v = PP[i, r, c] + RP[i, r]
            for j in range(4):
                TQ[i, j, pl.ds(8 * r, 8), :] = v[:, j * 128:(j + 1) * 128].astype(BF16)
    RQ[x, y] = TQ[x, y]
    qs = [remote(TQ.at[lax.rem(x + i, 4), lax.rem(y + j, 4)], RQ.at[x, y], dev(dx=i, dy=j))
          for i in range(4) for j in range(4) if (i, j) != (0, 0)]
    for r in qs:
        r.wait_recv()
    acc = RQ[0, 0].astype(F32)
    for i in range(1, 16):
        acc = acc + RQ[i // 4, i % 4].astype(F32)
    AZ[...] = acc.reshape(4, 8, 128)
    RZ[z] = AZ[zl]
    zs = [remote(AZ.at[lax.rem(zl + k, 4)], RZ.at[z], dev(dz=k)) for k in range(1, 8)]

    for r in wz:
        r.wait_recv()
    wc = remote(WG.at[:, :, c], WG.at[:, :, c], dev(core=oc))
    outs = []

    for r in gz:
        r.wait_recv()
    RG[z] = G2[z]
    g = RG[0].astype(F32)
    for i in range(1, 8):
        g = g + RG[i].astype(F32)
    G32[...] = g
    outs.append(localcopy(G32, o_g))
    wc.wait_recv()
    outs.append(localcopy(WG, o_wg))
    GG[x, zl, c] = g.astype(BF16)
    ga = [remote(GG.at[x, zl, c], GG.at[x, zl, c], dev(dzl=i)) for i in range(1, 4)]

    for r in zs:
        r.wait_recv()
    pj = RZ[0]
    for i in range(1, 8):
        pj = pj + RZ[i]
    for r in ga:
        r.wait_recv()
    gr = remote(GG.at[x, :, c], GG.at[x, :, c], dev(dx=1))
    gl = remote(GG.at[x, :, c], GG.at[x, :, c], dev(dx=3))
    gcs = [remote(GG.at[x, :, c], GG.at[x, :, c], dev(core=oc))]
    for r in ld_m:
        r.wait()
    ycol = pl.ds(pl.multiple_of(y * 128, 128), 128)
    first = 0.9 * MI[0, :, ycol] + 0.1 * pj
    second = 0.999 * MI[1, :, ycol] + 0.001 * pj * pj
    tilde = first / BIAS1 / (jnp.sqrt(second / BIAS2) + 1e-08)
    raw = jnp.sum(pj * pj, 0, keepdims=True)
    til = jnp.sum(tilde * tilde, 0, keepdims=True)
    r8 = lax.broadcasted_iota(jnp.int32, (8, 128), 0)
    VS[zl, c] = jnp.where(r8 == 0, raw, jnp.where(r8 == 1, til, 0.0))
    vs = [remote(VS.at[zl, c], VS.at[zl, c], dev(dzl=i, core=cc))
          for i, cc in ((2, c), (2, oc), (1, c), (3, c), (1, oc), (3, oc), (0, oc))]
    MO[y, 0] = first
    MO[y, 1] = second
    mo = [remote(MO.at[y], MO.at[y], dev(dy=i)) for i in range(1, 4)]
    for r in vs:
        r.wait_recv()
    v = VS[0, 0]
    for i in range(1, 8):
        v = v + VS[i // 2, i % 2]
    VX[x, y] = v
    vx = [remote(VX.at[x, y], VX.at[x, y], dev(dx=i, dy=j))
          for i, j in ((2, 2), (1, 2), (3, 2), (2, 1), (2, 3), (0, 2), (2, 0), (1, 1), (1, 3), (3, 1),
                       (3, 3), (0, 1), (0, 3), (1, 0), (3, 0))]
    for r in mo:
        r.wait_recv()
    outs.append(localcopy(MO, o_mo))
    xl, xr = lax.rem(x + 3, 4), lax.rem(x + 1, 4)
    lo, hi_ = pl.ds(0, 2), pl.ds(2, 2)
    gr.wait_recv()
    fr = remote(GG.at[xl, lo, c], GG.at[xl, lo, c], dev(dx=1))
    gcs.append(remote(GG.at[xl, :, c], GG.at[xl, :, c], dev(core=oc)))
    gl.wait_recv()
    fl = remote(GG.at[xr, hi_, c], GG.at[xr, hi_, c], dev(dx=3))
    gcs.append(remote(GG.at[xr, :, c], GG.at[xr, :, c], dev(core=oc)))
    for r in vx:
        r.wait_recv()
    for j in range(4):
        t = VX[0, j] + VX[1, j] + VX[2, j] + VX[3, j]
        col = 8.0 * (jnp.sqrt(t[1:2]) / jnp.sqrt(t[0:1] + 1e-06))
        CS[:, pl.ds(128 * j, 128)] = jnp.broadcast_to(col, (8, 128))
    outs.append(localcopy(CS, o_cs))
    xo = lax.rem(x + 2, 4)
    fr.wait_recv()
    gcs.append(remote(GG.at[xo, lo, c], GG.at[xo, lo, c], dev(core=oc)))
    fl.wait_recv()
    gcs.append(remote(GG.at[xo, hi_, c], GG.at[xo, hi_, c], dev(core=oc)))
    for r in gcs:
        r.wait_recv()
    outs.append(localcopy(GG, o_gg))
    for r in outs:
        r.wait()
    for r in copies:
        r.wait_send()


STEPS = 4
ROWS = 1024 // STEPS


def finish(wg, gg, g32, cs, mo, w32, o_qv, o_qs, o_nw, o_m1, o_m2):
    @pl.when(pl.program_id(0) == 0)
    def _():
        for j in range(4):
            cols = pl.ds(128 * j, 128)
            o_nw[:, cols] = w32[:, cols] - g32[:, cols] * cs[0:1, cols]
            o_m1[:, cols] = mo[j, 0]
            o_m2[:, cols] = mo[j, 1]

    eye = (lax.broadcasted_iota(jnp.int32, (8, 128), 0)
           == lax.broadcasted_iota(jnp.int32, (8, 128), 1)).astype(BF16)
    lane = lax.broadcasted_iota(jnp.int32, (128, 128), 1)
    for i in range(ROWS // 128):
        rows = pl.ds(i * 128, 128)
        packed = jnp.zeros((128, 128), F32)
        for j in range(4):
            cols = pl.ds(128 * j, 128)
            v = wg[rows, cols].astype(F32) - gg[rows, cols].astype(F32) * cs[0:1, cols]
            scale = (jnp.max(jnp.abs(v), 1, keepdims=True) + 1e-06).astype(BF16).astype(F32)
            o_qv[rows, cols] = (v * (1.0 / scale)).astype(BF16)
            packed = jnp.where(lane == j, scale, packed)
        tr = lax.dot_general(eye, packed.astype(BF16), (((1,), (1,)), ((), ())),
                             preferred_element_type=F32)
        o_qs[:, rows] = tr[:4].astype(BF16)


def shards(grad_values, grad_exponents, proj, weights, moment1, moment2):
    gv = grad_values.reshape(8, 4, 4, 2, 32, 512)
    ex = grad_exponents.reshape(4, 8192)
    any_ = pl.BlockSpec(memory_space=pl.ANY)
    V = pltpu.VMEM
    scratch = [
        V((2, 4, 2, 4, 4, 16, 512), BF16),
        V((2, 4, 2, 4, 4, 16, 512), BF16),
        V((2, 4, 2, 4, 4, 16, 512), BF16),
        V((2, 2, 4, 4, 16, 512), BF16),
        V((2, 2, 2, 4, 4, 16, 512), BF16),
        V((2, 4, 2, 4, 16, 512), BF16),
        V((2, 2, 4, 16, 512), BF16),
        V((2, 2, 2, 4, 16, 512), BF16),
        V((8, 32, 512), BF16),
        V((8, 32, 512), BF16),
        V((8, 32, 256), F32),
        V((3, 256, 256), BF16),
        V((4, 4, 2, 8, 512), F32),
        V((4, 4, 8, 512), F32),
        V((4, 4, 32, 128), BF16),
        V((4, 4, 32, 128), BF16),
        V((4, 8, 128), F32),
        V((8, 8, 128), F32),
        V((4, 2, 8, 128), F32),
        V((4, 2, 8, 128), F32),
        V((4, 4, 8, 128), F32),
        V((32, 512), F32),
        V((4, 4, 2, 32, 512), BF16),
        V((4, 4, 2, 32, 512), BF16),
        V((32, 512), F32),
        V((4, 8192), jnp.int32),
        V((4, 8192), jnp.int32),
        V((2, 8, 512), F32),
        V((8, 512), F32),
        V((128, 128), BF16),
        pltpu.SemaphoreType.DMA((NCOPY,)),
        pltpu.SemaphoreType.DMA((NCOPY,)),
        pltpu.SemaphoreType.DMA((40,)),
    ]
    wg, gg, g32, cs, mo = pl.pallas_call(
        kernel,
        out_shape=(
            jax.ShapeDtypeStruct((4, 4, 2, 32, 512), BF16),
            jax.ShapeDtypeStruct((4, 4, 2, 32, 512), BF16),
            jax.ShapeDtypeStruct((32, 512), F32),
            jax.ShapeDtypeStruct((8, 512), F32),
            jax.ShapeDtypeStruct((4, 2, 8, 128), F32),
        ),
        in_specs=[any_] * 6,
        out_specs=(any_,) * 5,
        scratch_shapes=scratch,
        compiler_params=pltpu.CompilerParams(
            collective_id=0, has_side_effects=True, vmem_limit_bytes=60 * 1024 * 1024
        ),
    )(gv, ex, proj, weights, moment1, moment2)
    whole = lambda *shape: pl.BlockSpec(shape, lambda i: (0,) * len(shape))
    return pl.pallas_call(
        finish,
        grid=(STEPS,),
        out_shape=(
            jax.ShapeDtypeStruct((1024, 512), BF16),
            jax.ShapeDtypeStruct((4, 1024), BF16),
            jax.ShapeDtypeStruct((32, 512), F32),
            jax.ShapeDtypeStruct((8, 512), F32),
            jax.ShapeDtypeStruct((8, 512), F32),
        ),
        in_specs=[
            pl.BlockSpec((ROWS, 512), lambda i: (i, 0)),
            pl.BlockSpec((ROWS, 512), lambda i: (i, 0)),
            whole(32, 512), whole(8, 512), whole(4, 2, 8, 128), whole(32, 512),
        ],
        out_specs=(
            pl.BlockSpec((ROWS, 512), lambda i: (i, 0)),
            pl.BlockSpec((4, ROWS), lambda i: (0, i)),
            whole(32, 512), whole(8, 512), whole(8, 512),
        ),
    )(wg.reshape(1024, 512), gg.reshape(1024, 512), g32, cs, mo, weights)


def solution(mesh):
    return jax.shard_map(
        shards,
        mesh=mesh,
        in_specs=(
            P(("node", "local"), None, None),
            P(("node", "local"), None, None),
            P(("local", "node"), None),
            P(("local", "node"), None),
            P("node", None),
            P("node", None),
        ),
        out_specs=(
            P("local", None),
            P(None, "local"),
            P(("local", "node"), None),
            P("node", None),
            P("node", None),
        ),
        check_vma=False,
    )
```

```python
import functools

import jax
import jax.numpy as jnp
from jax import lax
from jax.experimental import pallas as pl
from jax.experimental.pallas import tpu as pltpu
from jax.sharding import PartitionSpec as P

MESH = pl.DeviceIdType.MESH
BIAS1 = 1.0 - 0.9**10
BIAS2 = 1.0 - 0.999**10
F32 = jnp.float32
BF16 = jnp.bfloat16
NCOPY = 200
PRE = 16
XY = 384


def kernel(
    gv, ex, proj, wts, mom1, mom2,
    o_wg, o_gg, o_g, o_cs, o_mo,
    M0, M1, S, RA, RB, S2, RA2, RB2, G2, RG, PA, PT, PP, RP, TQ, RQ, AZ, RZ,
    MO, VS, VX, W32, WG, GG, G32, E0, E1, MI, CS, ONE,
    M0Z, M1Z, SZ, RR, RL, UZ, RAZ, RBZ, VZ, RY, GZ,
    ss, rs, ls,
):
    node = lax.axis_index("node")
    local = lax.axis_index("local")
    x = lax.div(node, 8)
    zl = lax.rem(lax.div(node, 2), 4)
    c = lax.rem(node, 2)
    zh = lax.div(local, 4)
    y = lax.rem(local, 4)
    z = zh * 4 + zl
    oc = 1 - c

    def dev(dx=0, dy=0, dz=0, core=None, dzl=None):
        xx = lax.rem(x + dx, 4)
        yy = lax.rem(y + dy, 4)
        if dzl is None:
            zz = lax.rem(z + dz, 8)
        else:
            zz = zh * 4 + lax.rem(zl + dzl, 4)
        cc = c if core is None else core
        return (xx * 8 + lax.rem(zz, 4) * 2 + cc, lax.div(zz, 4) * 4 + yy)

    counter = [0]
    copies = []

    def remote(src, dst, to):
        i = counter[0]
        counter[0] += 1
        r = pltpu.make_async_remote_copy(
            src_ref=src, dst_ref=dst, send_sem=ss.at[i], recv_sem=rs.at[i],
            device_id=to, device_id_type=MESH)
        r.start()
        copies.append(r)
        return r

    lcount = [0]

    def localcopy(src, dst):
        i = lcount[0]
        lcount[0] += 1
        r = pltpu.make_async_copy(src, dst, ls.at[i])
        r.start()
        return r

    partners = [dev(core=oc)]
    partners += [dev(dx=i, dy=j) for i in range(4) for j in range(4) if (i, j) != (0, 0)]
    partners += [dev(dz=k) for k in range(1, 8)]
    partners += [dev(dzl=k, core=oc) for k in range(1, 4)]
    barrier = pltpu.get_barrier_semaphore()
    for d in partners:
        pl.semaphore_signal(barrier, inc=1, device_id=d, device_id_type=MESH)

    REL = (2, 1, 3, 0)
    ORDER = ((0, 0), (0, 1), (1, 1), (2, 0), (1, 0), (2, 1), (3, 0), (3, 1))

    def dest(k, di):
        return lax.rem((x if k == 0 else y) + REL[di], 4)

    def gslice(k, di, h, core):
        d = dest(k, di)
        rows = pl.ds(16 * k, 16)
        if k == 0:
            return gv.at[pl.ds(h * 4, 4), d, :, core, rows, pl.ds(0, XY)]
        return gv.at[h * 4 + d, :, :, core, rows, pl.ds(0, XY)]

    def zslice(dz, core):
        t = lax.rem(z + dz, 8)
        return gv.at[pl.ds(lax.div(t, 4) * 4, 4), :, lax.rem(t, 4), core, :, pl.ds(XY, 128)]

    EVENTS = []
    for i, (di, h) in enumerate(ORDER):
        EVENTS += [(k, di, h) for k in range(2)]
        EVENTS += {1: [4], 3: [3, 5], 5: [2, 6], 7: [1, 7, 0]}.get(i, [])

    ld_e = localcopy(ex, E0)
    loads = {}
    for e in EVENTS:
        if isinstance(e, int):
            loads[e] = localcopy(zslice(e, c), M0Z.at[e])
        else:
            loads[e] = localcopy(gslice(*e, c), M0.at[e])
    ld_w = localcopy(wts, W32)
    ld_p = localcopy(proj, PA.at[z])
    ld_m = [localcopy(mom1, MI.at[0]), localcopy(mom2, MI.at[1])]
    ONE[...] = jnp.ones((128, 128), BF16)

    lane = lax.broadcasted_iota(jnp.int32, (32, 128), 1)
    row = lax.broadcasted_iota(jnp.int32, (32, 128), 0)
    hit0 = row + jnp.where(row >= 16, 48, 0) + c * 32
    masks = [lane == hit0, lane == hit0 + 16]

    def factors(E, k, di, h, q):
        d = dest(k, di)
        rows = []
        for u in range(2):
            for t in range(2):
                base = (((h * 4 + q + u) * 4 + d) if k == 0 else ((h * 4 + d) * 4 + q + u)) * 256 + t * 128
                e = E[:, pl.ds(pl.multiple_of(base, 128), 128)]
                f = 0.5 * lax.shift_left(jnp.ones_like(e), e + 1).astype(F32)
                rows += [jnp.where(masks[k], f[b:b + 1, :], 0.0).astype(BF16) for b in range(3)]
        return jnp.dot(jnp.concatenate(rows, 0), ONE[...], preferred_element_type=F32).astype(BF16)

    def dequant(k, di, h, E, M, add):
        def body(p, carry):
            q = p * 2
            fac = factors(E, k, di, h, q)
            for u in range(2):
                for t in range(2):
                    for b in range(3):
                        for zz in range(2):
                            cols = pl.ds(b * 128, 128)
                            r0 = (((u * 2 + t) * 3 + b) * 2 + zz) * 16
                            v = M[k, di, h, q + u, 2 * t + zz, :, cols] * fac[r0:r0 + 16]
                            if add:
                                v = S[k, di, h, q + u, 2 * t + zz, :, cols] + v
                            S[k, di, h, q + u, 2 * t + zz, :, cols] = v
            return carry

        lax.fori_loop(0, 2, body, 0)

    def dequant_z(dz, E, M, add):
        t = lax.rem(z + dz, 8)
        th, tl = lax.div(t, 4), lax.rem(t, 4)
        mask = lane == row + lax.rem(tl, 2) * 64 + c * 32

        def body(p, carry):
            rows = []
            for u in range(8):
                base = ((th * 4 + p * 2 + u // 4) * 4 + u % 4) * 256 + lax.div(tl, 2) * 128
                e = E[:, pl.ds(pl.multiple_of(base, 128), 128)]
                f = 0.5 * lax.shift_left(jnp.ones_like(e), e + 1).astype(F32)
                rows.append(jnp.where(mask, f[3:4, :], 0.0).astype(BF16))
            fac = jnp.dot(jnp.concatenate(rows, 0), ONE[...], preferred_element_type=F32).astype(BF16)
            for u in range(8):
                at = (dz, p * 2 + u // 4, u % 4)
                v = M[at] * fac[u * 32:u * 32 + 32]
                if add:
                    v = SZ[at] + v
                SZ[at] = v
            return carry

        lax.fori_loop(0, 2, body, 0)

    def prepass(e):
        loads[e].wait()
        if isinstance(e, int):
            dequant_z(e, E0, M0Z, False)
        else:
            dequant(*e, E0, M0, False)

    ld_w.wait()
    WG[x, zl, c] = W32[...].astype(BF16)
    ld_e.wait()
    G2[:, :, pl.ds(XY, 128)] = jnp.zeros((8, 32, 128), BF16)
    for e in EVENTS[:PRE]:
        prepass(e)

    pl.semaphore_wait(barrier, len(partners))

    sendE = remote(ex, E1, dev(core=oc))
    sends = {}
    for e in EVENTS:
        if isinstance(e, int):
            sends[e] = remote(zslice(e, oc), M1Z.at[e], dev(core=oc))
        else:
            sends[e] = remote(gslice(*e, oc), M1.at[e], dev(core=oc))
    wz = [remote(WG.at[x, zl, c], WG.at[x, zl, c], dev(dzl=i)) for i in range(1, 4)]
    pas = [remote(proj, PA.at[z], dev(dz=k)) for k in range(1, 8)]

    def nb(k, stage, step):
        if (k + stage) % 2 == 0:
            return dev(dx=step)
        return dev(dy=step)

    for e in EVENTS[PRE:]:
        prepass(e)
    sendE.wait_recv()
    RAc, RBc = {}, {}

    def addinto(dst, src):
        def body(i, carry):
            q, r = lax.div(i, 4), lax.rem(i, 4)
            dst[q, r] = dst[q, r] + src[q, r]
            return carry
        lax.fori_loop(0, 16, body, 0, unroll=4)

    def zadd(dz, src, ys):
        def body(i, carry):
            SZ[dz, i] = SZ[dz, i] + src[i]
            return carry
        lax.fori_loop(ys[0], ys[1], body, 0)

    zright, zleft = dev(dz=1), dev(dz=7)
    HALF = (pl.ds(0, 2), pl.ds(2, 2))

    def wait_for(r, ref):
        r.wait_recv()
        return ref

    for e in EVENTS:
        sends[e].wait_recv()
        if isinstance(e, int):
            dequant_z(e, E1, M1Z, True)
            if e == 4:
                z4 = [remote(SZ.at[4, HALF[0]], RR.at[0, HALF[0]], zright),
                      remote(SZ.at[4, HALF[1]], RL.at[0, HALF[1]], zleft)]
            elif e == 3:
                z3 = remote(SZ.at[3, HALF[1]], RR.at[1, HALF[1]], zright)
            elif e == 5:
                z5 = remote(SZ.at[5, HALF[0]], RL.at[1, HALF[0]], zleft)
            elif e == 6:
                zadd(3, wait_for(z4[0], RR.at[0]), (0, 2))
                z3b = remote(SZ.at[3, HALF[0]], RR.at[1, HALF[0]], zright)
                zadd(5, wait_for(z4[1], RL.at[0]), (2, 4))
                z5b = remote(SZ.at[5, HALF[1]], RL.at[1, HALF[1]], zleft)
            continue
        k, di, h = e
        dequant(k, di, h, E1, M1, True)
        step = 1 if h == 0 else 3
        if di == 0:
            RAc[k, h] = remote(S.at[k, 0, h], RA.at[k, h], nb(k, 0, step))
        elif (di, h) == (1, 1):
            RBc[k, 0, 1] = remote(S.at[k, 1, 1], RB.at[k, 0, 1], nb(k, 0, 1))
        elif (di, h) == (2, 0):
            RBc[k, 1, 0] = remote(S.at[k, 2, 0], RB.at[k, 1, 0], nb(k, 0, 3))
    for h in range(2):
        for k in range(2):
            RAc[k, h].wait_recv()
            di = 1 if h == 0 else 2
            addinto(S.at[k, di, h], RA.at[k, h])
            if h == 0:
                RBc[k, 0, 0] = remote(S.at[k, 1, 0], RB.at[k, 0, 0], nb(k, 0, 1))
            else:
                RBc[k, 1, 1] = remote(S.at[k, 2, 1], RB.at[k, 1, 1], nb(k, 0, 3))
    z3.wait_recv()
    zadd(2, wait_for(z3b, RR.at[1]), (0, 4))
    z2 = remote(SZ.at[2], RR.at[2], zright)
    z5.wait_recv()
    zadd(6, wait_for(z5b, RL.at[1]), (0, 4))
    z6 = remote(SZ.at[6], RL.at[2], zleft)

    ld_p.wait()
    for r in pas:
        r.wait_recv()
    pt = jnp.transpose(PA[...].reshape(256, 256))
    hi = pt.astype(BF16)
    rest = pt - hi.astype(F32)
    mid = rest.astype(BF16)
    PT[0] = hi
    PT[1] = mid
    PT[2] = (rest - mid.astype(F32)).astype(BF16)

    zadd(1, wait_for(z2, RR.at[2]), (0, 4))
    z1 = remote(SZ.at[1], RR.at[3], zright)
    zadd(7, wait_for(z6, RL.at[2]), (0, 4))
    z7 = remote(SZ.at[7], RL.at[3], zleft)

    RAc2, RBc2 = {}, {}

    def finish1(k, di, h):
        a = lax.rem((y if k == 0 else x) + REL[di], 4)
        for r in range(4):
            v = (S[k, 3, h, a, r].astype(F32) + RB[k, 0, h, a, r].astype(F32)
                 + RB[k, 1, h, a, r].astype(F32))
            S2[k, di, h, r] = v.astype(BF16)

    for k in range(2):
        for s in range(2):
            for h in ((1, 0) if s == 0 else (0, 1)):
                RBc[k, s, h].wait_recv()
    for di, h in ORDER:
        for k in range(2):
            finish1(k, di, h)
            step = 1 if h == 0 else 3
            if di == 0:
                RAc2[k, h] = remote(S2.at[k, 0, h], RA2.at[k, h], nb(k, 1, step))
            elif (di, h) == (1, 1):
                RBc2[k, 0, 1] = remote(S2.at[k, 1, 1], RB2.at[k, 0, 1], nb(k, 1, 1))
            elif (di, h) == (2, 0):
                RBc2[k, 1, 0] = remote(S2.at[k, 2, 0], RB2.at[k, 1, 0], nb(k, 1, 3))
    z1.wait_recv()
    z7.wait_recv()
    for i in range(4):
        t = lax.rem(x + REL[i], 4)
        for j in range(4):
            UZ[i, j] = (SZ[0, j, t].astype(F32) + RR[3, j, t].astype(F32)
                        + RL[3, j, t].astype(F32)).astype(BF16)
    za = [remote(UZ.at[0, HALF[0]], RAZ.at[0], dev(dx=1)), remote(UZ.at[0, HALF[1]], RAZ.at[1], dev(dx=3))]
    zb = [remote(UZ.at[1, HALF[1]], RBZ.at[0, HALF[1]], dev(dx=1)),
          remote(UZ.at[2, HALF[0]], RBZ.at[1, HALF[0]], dev(dx=3))]
    for h in range(2):
        for k in range(2):
            RAc2[k, h].wait_recv()
            di = 1 if h == 0 else 2
            for r in range(4):
                S2[k, di, h, r] = S2[k, di, h, r] + RA2[k, h, r]
            if h == 0:
                RBc2[k, 0, 0] = remote(S2.at[k, 1, 0], RB2.at[k, 0, 0], nb(k, 1, 1))
            else:
                RBc2[k, 1, 1] = remote(S2.at[k, 2, 1], RB2.at[k, 1, 1], nb(k, 1, 3))
    za[0].wait_recv()
    UZ[1, HALF[0]] = UZ[1, HALF[0]] + RAZ[0]
    zb.append(remote(UZ.at[1, HALF[0]], RBZ.at[0, HALF[0]], dev(dx=1)))
    za[1].wait_recv()
    UZ[2, HALF[1]] = UZ[2, HALF[1]] + RAZ[1]
    zb.append(remote(UZ.at[2, HALF[1]], RBZ.at[1, HALF[1]], dev(dx=3)))
    for k in range(2):
        for s in range(2):
            for h in ((1, 0) if s == 0 else (0, 1)):
                RBc2[k, s, h].wait_recv()
        for h in range(2):
            for r in range(4):
                v = (S2[k, 3, h, r].astype(F32) + RB2[k, 0, h, r].astype(F32)
                     + RB2[k, 1, h, r].astype(F32))
                G2[h * 4 + r, pl.ds(16 * k, 16), pl.ds(0, XY)] = v.astype(BF16)

    for r in zb:
        r.wait_recv()
    VZ[...] = (UZ[3].astype(F32) + RBZ[0].astype(F32) + RBZ[1].astype(F32)).astype(BF16)
    zy = [remote(VZ.at[lax.rem(y + i, 4)], RY.at[y], dev(dy=i)) for i in (2, 1, 3)]
    gz = [remote(G2.at[lax.rem(z + k, 8), :, pl.ds(0, XY)], RG.at[z], dev(dz=k)) for k in (4, 3, 5, 2, 6, 1, 7)]
    RY[y] = VZ[y]
    for r in zy:
        r.wait_recv()
    gz_own = RY[0].astype(F32) + RY[1].astype(F32) + RY[2].astype(F32) + RY[3].astype(F32)
    GZ[...] = gz_own
    G2[z, :, pl.ds(XY, 128)] = gz_own.astype(BF16)

    g2 = G2[...].reshape(256, 512)
    part = (jnp.dot(PT[0], g2, preferred_element_type=F32)
            + jnp.dot(PT[1], g2, preferred_element_type=F32)
            + jnp.dot(PT[2], g2, preferred_element_type=F32))
    PP[...] = part.reshape(4, 4, 2, 8, 512)
    pc = remote(PP.at[:, :, oc], RP, dev(core=oc))
    pc.wait_recv()
    for i in range(4):
        for r in range(4):
            v = PP[i, r, c] + RP[i, r]
            for j in range(4):
                TQ[i, j, pl.ds(8 * r, 8), :] = v[:, j * 128:(j + 1) * 128].astype(BF16)
    RQ[x, y] = TQ[x, y]
    qs = [remote(TQ.at[lax.rem(x + i, 4), lax.rem(y + j, 4)], RQ.at[x, y], dev(dx=i, dy=j))
          for i in range(4) for j in range(4) if (i, j) != (0, 0)]
    for r in qs:
        r.wait_recv()
    acc = RQ[0, 0].astype(F32)
    for i in range(1, 16):
        acc = acc + RQ[i // 4, i % 4].astype(F32)
    AZ[...] = acc.reshape(4, 8, 128)
    RZ[z] = AZ[zl]
    zs = [remote(AZ.at[lax.rem(zl + k, 4)], RZ.at[z], dev(dz=k)) for k in range(1, 8)]

    xl, xr, xo = lax.rem(x + 3, 4), lax.rem(x + 1, 4), lax.rem(x + 2, 4)

    class Gather:
        def __init__(g, B):
            g.B, g.cs = B, []
            g.r, g.l = g.send(x, slice(None), 1), g.send(x, slice(None), 3)
            g.core(x, slice(None))

        def send(g, i, part, step):
            v = g.B.at[i, :, c] if part == slice(None) else g.B.at[i, part, c]
            return remote(v, v, dev(dx=step))

        def core(g, i, part):
            v = g.B.at[i, :, c] if part == slice(None) else g.B.at[i, part, c]
            g.cs.append(remote(v, v, dev(core=oc)))

        def forward(g):
            g.r.wait_recv()
            g.fr = g.send(xl, HALF[0], 1)
            g.core(xl, slice(None))
            g.l.wait_recv()
            g.fl = g.send(xr, HALF[1], 3)
            g.core(xr, slice(None))

        def end(g):
            g.fr.wait_recv()
            g.core(xo, HALF[0])
            g.fl.wait_recv()
            g.core(xo, HALF[1])
            for r in g.cs:
                r.wait_recv()

    for r in wz:
        r.wait_recv()
    wgather = Gather(WG)
    outs = []

    for r in gz:
        r.wait_recv()
    RG[z] = G2[z, :, pl.ds(0, XY)]
    g = RG[0].astype(F32)
    for i in range(1, 8):
        g = g + RG[i].astype(F32)
    G32[:, pl.ds(0, XY)] = g
    G32[:, pl.ds(XY, 128)] = GZ[...]
    outs.append(localcopy(G32, o_g))
    GG[x, zl, c, :, pl.ds(0, XY)] = g.astype(BF16)
    GG[x, zl, c, :, pl.ds(XY, 128)] = GZ[...].astype(BF16)
    ga = [remote(GG.at[x, zl, c], GG.at[x, zl, c], dev(dzl=i)) for i in range(1, 4)]

    for r in zs:
        r.wait_recv()
    pj = RZ[0]
    for i in range(1, 8):
        pj = pj + RZ[i]
    for r in ga:
        r.wait_recv()
    wgather.forward()
    ggather = Gather(GG)
    for r in ld_m:
        r.wait()
    ycol = pl.ds(pl.multiple_of(y * 128, 128), 128)
    first = 0.9 * MI[0, :, ycol] + 0.1 * pj
    second = 0.999 * MI[1, :, ycol] + 0.001 * pj * pj
    tilde = first / BIAS1 / (jnp.sqrt(second / BIAS2) + 1e-08)
    raw = jnp.sum(pj * pj, 0, keepdims=True)
    til = jnp.sum(tilde * tilde, 0, keepdims=True)
    r8 = lax.broadcasted_iota(jnp.int32, (8, 128), 0)
    VS[zl, c] = jnp.where(r8 == 0, raw, jnp.where(r8 == 1, til, 0.0))
    vs = [remote(VS.at[zl, c], VS.at[zl, c], dev(dzl=i, core=cc))
          for i, cc in ((2, c), (2, oc), (1, c), (3, c), (1, oc), (3, oc), (0, oc))]
    MO[y, 0] = first
    MO[y, 1] = second
    mo = [remote(MO.at[y], MO.at[y], dev(dy=i)) for i in range(1, 4)]
    for r in vs:
        r.wait_recv()
    v = VS[0, 0]
    for i in range(1, 8):
        v = v + VS[i // 2, i % 2]
    VX[x, y] = v
    vx = [remote(VX.at[x, y], VX.at[x, y], dev(dx=i, dy=j))
          for i, j in ((2, 2), (1, 2), (3, 2), (2, 1), (2, 3), (0, 2), (2, 0), (1, 1), (1, 3), (3, 1),
                       (3, 3), (0, 1), (0, 3), (1, 0), (3, 0))]
    for r in mo:
        r.wait_recv()
    outs.append(localcopy(MO, o_mo))
    wgather.end()
    outs.append(localcopy(WG, o_wg))
    ggather.forward()
    for r in vx:
        r.wait_recv()
    for j in range(4):
        t = VX[0, j] + VX[1, j] + VX[2, j] + VX[3, j]
        col = 8.0 * (jnp.sqrt(t[1:2]) / jnp.sqrt(t[0:1] + 1e-06))
        CS[:, pl.ds(128 * j, 128)] = jnp.broadcast_to(col, (8, 128))
    outs.append(localcopy(CS, o_cs))
    ggather.end()
    outs.append(localcopy(GG, o_gg))
    for r in outs:
        r.wait()
    for r in copies:
        r.wait_send()


STEPS = 4
ROWS = 1024 // STEPS


def finish(wg, gg, g32, cs, mo, w32, o_qv, o_qs, o_nw, o_m1, o_m2):
    @pl.when(pl.program_id(0) == 0)
    def _():
        for j in range(4):
            cols = pl.ds(128 * j, 128)
            o_nw[:, cols] = w32[:, cols] - g32[:, cols] * cs[0:1, cols]
            o_m1[:, cols] = mo[j, 0]
            o_m2[:, cols] = mo[j, 1]

    eye = (lax.broadcasted_iota(jnp.int32, (8, 128), 0)
           == lax.broadcasted_iota(jnp.int32, (8, 128), 1)).astype(BF16)
    lane = lax.broadcasted_iota(jnp.int32, (128, 128), 1)
    for i in range(ROWS // 128):
        rows = pl.ds(i * 128, 128)
        packed = jnp.zeros((128, 128), F32)
        for j in range(4):
            cols = pl.ds(128 * j, 128)
            v = wg[rows, cols].astype(F32) - gg[rows, cols].astype(F32) * cs[0:1, cols]
            scale = (jnp.max(jnp.abs(v), 1, keepdims=True) + 1e-06).astype(BF16).astype(F32)
            o_qv[rows, cols] = (v * (1.0 / scale)).astype(BF16)
            packed = jnp.where(lane == j, scale, packed)
        tr = lax.dot_general(eye, packed.astype(BF16), (((1,), (1,)), ((), ())),
                             preferred_element_type=F32)
        o_qs[:, rows] = tr[:4].astype(BF16)


def shards(grad_values, grad_exponents, proj, weights, moment1, moment2):
    gv = grad_values.reshape(8, 4, 4, 2, 32, 512)
    ex = grad_exponents.reshape(4, 8192)
    any_ = pl.BlockSpec(memory_space=pl.ANY)
    V = pltpu.VMEM
    scratch = [
        V((2, 4, 2, 4, 4, 16, XY), BF16),
        V((2, 4, 2, 4, 4, 16, XY), BF16),
        V((2, 4, 2, 4, 4, 16, XY), BF16),
        V((2, 2, 4, 4, 16, XY), BF16),
        V((2, 2, 2, 4, 4, 16, XY), BF16),
        V((2, 4, 2, 4, 16, XY), BF16),
        V((2, 2, 4, 16, XY), BF16),
        V((2, 2, 2, 4, 16, XY), BF16),
        V((8, 32, 512), BF16),
        V((8, 32, XY), BF16),
        V((8, 32, 256), F32),
        V((3, 256, 256), BF16),
        V((4, 4, 2, 8, 512), F32),
        V((4, 4, 8, 512), F32),
        V((4, 4, 32, 128), BF16),
        V((4, 4, 32, 128), BF16),
        V((4, 8, 128), F32),
        V((8, 8, 128), F32),
        V((4, 2, 8, 128), F32),
        V((4, 2, 8, 128), F32),
        V((4, 4, 8, 128), F32),
        V((32, 512), F32),
        V((4, 4, 2, 32, 512), BF16),
        V((4, 4, 2, 32, 512), BF16),
        V((32, 512), F32),
        V((4, 8192), jnp.int32),
        V((4, 8192), jnp.int32),
        V((2, 8, 512), F32),
        V((8, 512), F32),
        V((128, 128), BF16),
        V((8, 4, 4, 32, 128), BF16),
        V((8, 4, 4, 32, 128), BF16),
        V((8, 4, 4, 32, 128), BF16),
        V((4, 4, 4, 32, 128), BF16),
        V((4, 4, 4, 32, 128), BF16),
        V((4, 4, 32, 128), BF16),
        V((2, 2, 32, 128), BF16),
        V((2, 4, 32, 128), BF16),
        V((4, 32, 128), BF16),
        V((4, 32, 128), BF16),
        V((32, 128), F32),
        pltpu.SemaphoreType.DMA((NCOPY,)),
        pltpu.SemaphoreType.DMA((NCOPY,)),
        pltpu.SemaphoreType.DMA((48,)),
    ]
    wg, gg, g32, cs, mo = pl.pallas_call(
        kernel,
        out_shape=(
            jax.ShapeDtypeStruct((4, 4, 2, 32, 512), BF16),
            jax.ShapeDtypeStruct((4, 4, 2, 32, 512), BF16),
            jax.ShapeDtypeStruct((32, 512), F32),
            jax.ShapeDtypeStruct((8, 512), F32),
            jax.ShapeDtypeStruct((4, 2, 8, 128), F32),
        ),
        in_specs=[any_] * 6,
        out_specs=(any_,) * 5,
        scratch_shapes=scratch,
        compiler_params=pltpu.CompilerParams(
            collective_id=0, has_side_effects=True, vmem_limit_bytes=60 * 1024 * 1024
        ),
    )(gv, ex, proj, weights, moment1, moment2)
    whole = lambda *shape: pl.BlockSpec(shape, lambda i: (0,) * len(shape))
    return pl.pallas_call(
        finish,
        grid=(STEPS,),
        out_shape=(
            jax.ShapeDtypeStruct((1024, 512), BF16),
            jax.ShapeDtypeStruct((4, 1024), BF16),
            jax.ShapeDtypeStruct((32, 512), F32),
            jax.ShapeDtypeStruct((8, 512), F32),
            jax.ShapeDtypeStruct((8, 512), F32),
        ),
        in_specs=[
            pl.BlockSpec((ROWS, 512), lambda i: (i, 0)),
            pl.BlockSpec((ROWS, 512), lambda i: (i, 0)),
            whole(32, 512), whole(8, 512), whole(4, 2, 8, 128), whole(32, 512),
        ],
        out_specs=(
            pl.BlockSpec((ROWS, 512), lambda i: (i, 0)),
            pl.BlockSpec((4, ROWS), lambda i: (0, i)),
            whole(32, 512), whole(8, 512), whole(8, 512),
        ),
    )(wg.reshape(1024, 512), gg.reshape(1024, 512), g32, cs, mo, weights)


def solution(mesh):
    return jax.shard_map(
        shards,
        mesh=mesh,
        in_specs=(
            P(("node", "local"), None, None),
            P(("node", "local"), None, None),
            P(("local", "node"), None),
            P(("local", "node"), None),
            P("node", None),
            P("node", None),
        ),
        out_specs=(
            P("local", None),
            P(None, "local"),
            P(("local", "node"), None),
            P("node", None),
            P("node", None),
        ),
        check_vma=False,
    )
```

```python
import functools

import jax
import jax.numpy as jnp
from jax import lax
from jax.experimental import pallas as pl
from jax.experimental.pallas import tpu as pltpu
from jax.sharding import PartitionSpec as P

MESH = pl.DeviceIdType.MESH
BIAS1 = 1.0 - 0.9**10
BIAS2 = 1.0 - 0.999**10
F32 = jnp.float32
BF16 = jnp.bfloat16
NCOPY = 160
PRE = 10


def kernel(
    gv, ex, proj, wts, mom1, mom2,
    o_wg, o_gg, o_g, o_cs, o_mo,
    M0, M1, S, RA, RB, S2, RA2, RB2, G2, RG, PA, PT, PP, RP, TQ, RQ, AZ, RZ,
    MO, VS, VX, W32, WG, GG, G32, E0, E1, MI, CS, ONE,
    ss, rs, ls,
):
    node = lax.axis_index("node")
    local = lax.axis_index("local")
    x = lax.div(node, 8)
    zl = lax.rem(lax.div(node, 2), 4)
    c = lax.rem(node, 2)
    zh = lax.div(local, 4)
    y = lax.rem(local, 4)
    z = zh * 4 + zl
    oc = 1 - c

    def dev(dx=0, dy=0, dz=0, core=None, dzl=None):
        xx = lax.rem(x + dx, 4)
        yy = lax.rem(y + dy, 4)
        if dzl is None:
            zz = lax.rem(z + dz, 8)
        else:
            zz = zh * 4 + lax.rem(zl + dzl, 4)
        cc = c if core is None else core
        return (xx * 8 + lax.rem(zz, 4) * 2 + cc, lax.div(zz, 4) * 4 + yy)

    counter = [0]
    copies = []

    def remote(src, dst, to):
        i = counter[0]
        counter[0] += 1
        r = pltpu.make_async_remote_copy(
            src_ref=src, dst_ref=dst, send_sem=ss.at[i], recv_sem=rs.at[i],
            device_id=to, device_id_type=MESH)
        r.start()
        copies.append(r)
        return r

    lcount = [0]

    def localcopy(src, dst):
        i = lcount[0]
        lcount[0] += 1
        r = pltpu.make_async_copy(src, dst, ls.at[i])
        r.start()
        return r

    partners = [dev(core=oc)]
    partners += [dev(dx=i, dy=j) for i in range(4) for j in range(4) if (i, j) != (0, 0)]
    partners += [dev(dz=k) for k in range(1, 8)]
    partners += [dev(dzl=k, core=oc) for k in range(1, 4)]
    barrier = pltpu.get_barrier_semaphore()
    for d in partners:
        pl.semaphore_signal(barrier, inc=1, device_id=d, device_id_type=MESH)

    REL = (2, 1, 3, 0)
    ORDER = ((0, 0), (0, 1), (1, 1), (2, 0), (1, 0), (2, 1), (3, 0), (3, 1))

    def dest(k, di):
        return lax.rem((x if k == 0 else y) + REL[di], 4)

    def gslice(k, di, h, core):
        d = dest(k, di)
        rows = pl.ds(16 * k, 16)
        if k == 0:
            return gv.at[pl.ds(h * 4, 4), d, :, core, rows, :]
        return gv.at[h * 4 + d, :, :, core, rows, :]

    ld_e = localcopy(ex, E0)
    loads = {}
    for di, h in ORDER:
        for k in range(2):
            loads[k, di, h] = localcopy(gslice(k, di, h, c), M0.at[k, di, h])
    ld_w = localcopy(wts, W32)
    ld_p = localcopy(proj, PA.at[z])
    ld_m = [localcopy(mom1, MI.at[0]), localcopy(mom2, MI.at[1])]
    ONE[...] = jnp.ones((128, 128), BF16)

    lane = lax.broadcasted_iota(jnp.int32, (32, 128), 1)
    row = lax.broadcasted_iota(jnp.int32, (32, 128), 0)
    hit0 = row + jnp.where(row >= 16, 48, 0) + c * 32
    masks = [lane == hit0, lane == hit0 + 16]

    def factors(E, k, di, h, q):
        d = dest(k, di)
        rows = []
        for u in range(2):
            for t in range(2):
                base = (((h * 4 + q + u) * 4 + d) if k == 0 else ((h * 4 + d) * 4 + q + u)) * 256 + t * 128
                e = E[:, pl.ds(pl.multiple_of(base, 128), 128)]
                f = 0.5 * lax.shift_left(jnp.ones_like(e), e + 1).astype(F32)
                rows += [jnp.where(masks[k], f[b:b + 1, :], 0.0).astype(BF16) for b in range(4)]
        return jnp.dot(jnp.concatenate(rows, 0), ONE[...], preferred_element_type=F32).astype(BF16)

    def dequant(k, di, h, E, M, add):
        def body(p, carry):
            q = p * 2
            fac = factors(E, k, di, h, q)
            for u in range(2):
                for t in range(2):
                    for b in range(4):
                        for zz in range(2):
                            cols = pl.ds(b * 128, 128)
                            r0 = (((u * 2 + t) * 4 + b) * 2 + zz) * 16
                            v = M[k, di, h, q + u, 2 * t + zz, :, cols] * fac[r0:r0 + 16]
                            if add:
                                v = S[k, di, h, q + u, 2 * t + zz, :, cols] + v
                            S[k, di, h, q + u, 2 * t + zz, :, cols] = v
            return carry

        lax.fori_loop(0, 2, body, 0)

    ld_w.wait()
    WG[x, zl, c] = W32[...].astype(BF16)
    ld_e.wait()
    UNITS = [(k, di, h) for di, h in ORDER for k in range(2)]
    for n, (k, di, h) in enumerate(UNITS):
        if n == PRE:
            break
        loads[k, di, h].wait()
        dequant(k, di, h, E0, M0, False)

    pl.semaphore_wait(barrier, len(partners))

    sendE = remote(ex, E1, dev(core=oc))
    wx = [remote(WG.at[x, zl, c], WG.at[x, zl, c], dev(dx=i)) for i in range(1, 4)]
    sends = {}
    for di, h in ORDER:
        for k in range(2):
            sends[k, di, h] = remote(gslice(k, di, h, oc), M1.at[k, di, h], dev(core=oc))
    pas = [remote(proj, PA.at[z], dev(dz=k)) for k in range(1, 8)]

    def nb(k, stage, step):
        if (k + stage) % 2 == 0:
            return dev(dx=step)
        return dev(dy=step)

    for k, di, h in UNITS[PRE:]:
        loads[k, di, h].wait()
        dequant(k, di, h, E0, M0, False)
    sendE.wait_recv()
    RAc, RBc = {}, {}

    def addinto(dst, src):
        def body(i, carry):
            q, r = lax.div(i, 4), lax.rem(i, 4)
            dst[q, r] = dst[q, r] + src[q, r]
            return carry
        lax.fori_loop(0, 16, body, 0, unroll=4)

    for n, (di, h) in enumerate(ORDER):
        for k in range(2):
            sends[k, di, h].wait_recv()
            dequant(k, di, h, E1, M1, True)
            step = 1 if h == 0 else 3
            if di == 0:
                RAc[k, h] = remote(S.at[k, 0, h], RA.at[k, h], nb(k, 0, step))
            elif (di, h) == (1, 1):
                RBc[k, 0, 1] = remote(S.at[k, 1, 1], RB.at[k, 0, 1], nb(k, 0, 1))
            elif (di, h) == (2, 0):
                RBc[k, 1, 0] = remote(S.at[k, 2, 0], RB.at[k, 1, 0], nb(k, 0, 3))
        if n == 3:
            for r in wx:
                r.wait_recv()
            wz = [remote(WG.at[:, zl, c], WG.at[:, zl, c], dev(dzl=i)) for i in range(1, 4)]
    for h in range(2):
        for k in range(2):
            RAc[k, h].wait_recv()
            di = 1 if h == 0 else 2
            addinto(S.at[k, di, h], RA.at[k, h])
            if h == 0:
                RBc[k, 0, 0] = remote(S.at[k, 1, 0], RB.at[k, 0, 0], nb(k, 0, 1))
            else:
                RBc[k, 1, 1] = remote(S.at[k, 2, 1], RB.at[k, 1, 1], nb(k, 0, 3))


    ld_p.wait()
    for r in pas:
        r.wait_recv()
    pt = jnp.transpose(PA[...].reshape(256, 256))
    hi = pt.astype(BF16)
    rest = pt - hi.astype(F32)
    mid = rest.astype(BF16)
    PT[0] = hi
    PT[1] = mid
    PT[2] = (rest - mid.astype(F32)).astype(BF16)

    RAc2, RBc2 = {}, {}

    def finish1(k, di, h):
        a = lax.rem((y if k == 0 else x) + REL[di], 4)
        for r in range(4):
            v = (S[k, 3, h, a, r].astype(F32) + RB[k, 0, h, a, r].astype(F32)
                 + RB[k, 1, h, a, r].astype(F32))
            S2[k, di, h, r] = v.astype(BF16)

    for k in range(2):
        for s in range(2):
            for h in ((1, 0) if s == 0 else (0, 1)):
                RBc[k, s, h].wait_recv()
    for di, h in ORDER:
        for k in range(2):
            finish1(k, di, h)
            step = 1 if h == 0 else 3
            if di == 0:
                RAc2[k, h] = remote(S2.at[k, 0, h], RA2.at[k, h], nb(k, 1, step))
            elif (di, h) == (1, 1):
                RBc2[k, 0, 1] = remote(S2.at[k, 1, 1], RB2.at[k, 0, 1], nb(k, 1, 1))
            elif (di, h) == (2, 0):
                RBc2[k, 1, 0] = remote(S2.at[k, 2, 0], RB2.at[k, 1, 0], nb(k, 1, 3))
    for h in range(2):
        for k in range(2):
            RAc2[k, h].wait_recv()
            di = 1 if h == 0 else 2
            for r in range(4):
                S2[k, di, h, r] = S2[k, di, h, r] + RA2[k, h, r]
            if h == 0:
                RBc2[k, 0, 0] = remote(S2.at[k, 1, 0], RB2.at[k, 0, 0], nb(k, 1, 1))
            else:
                RBc2[k, 1, 1] = remote(S2.at[k, 2, 1], RB2.at[k, 1, 1], nb(k, 1, 3))
    for k in range(2):
        for s in range(2):
            for h in ((1, 0) if s == 0 else (0, 1)):
                RBc2[k, s, h].wait_recv()
        for h in range(2):
            for r in range(4):
                v = (S2[k, 3, h, r].astype(F32) + RB2[k, 0, h, r].astype(F32)
                     + RB2[k, 1, h, r].astype(F32))
                G2[h * 4 + r, pl.ds(16 * k, 16), :] = v.astype(BF16)

    gz = [remote(G2.at[lax.rem(z + k, 8)], RG.at[z], dev(dz=k)) for k in (4, 3, 5, 2, 6, 1, 7)]

    g2 = G2[...].reshape(256, 512)
    part = (jnp.dot(PT[0], g2, preferred_element_type=F32)
            + jnp.dot(PT[1], g2, preferred_element_type=F32)
            + jnp.dot(PT[2], g2, preferred_element_type=F32))
    PP[...] = part.reshape(4, 4, 2, 8, 512)
    pc = remote(PP.at[:, :, oc], RP, dev(core=oc))
    pc.wait_recv()
    for i in range(4):
        for r in range(4):
            v = PP[i, r, c] + RP[i, r]
            for j in range(4):
                TQ[i, j, pl.ds(8 * r, 8), :] = v[:, j * 128:(j + 1) * 128].astype(BF16)
    RQ[x, y] = TQ[x, y]
    qs = [remote(TQ.at[lax.rem(x + i, 4), lax.rem(y + j, 4)], RQ.at[x, y], dev(dx=i, dy=j))
          for i in range(4) for j in range(4) if (i, j) != (0, 0)]
    for r in qs:
        r.wait_recv()
    acc = RQ[0, 0].astype(F32)
    for i in range(1, 16):
        acc = acc + RQ[i // 4, i % 4].astype(F32)
    AZ[...] = acc.reshape(4, 8, 128)
    RZ[z] = AZ[zl]
    zs = [remote(AZ.at[lax.rem(zl + k, 4)], RZ.at[z], dev(dz=k)) for k in range(1, 8)]

    for r in wz:
        r.wait_recv()
    wc = remote(WG.at[:, :, c], WG.at[:, :, c], dev(core=oc))
    outs = []

    for r in gz:
        r.wait_recv()
    RG[z] = G2[z]
    g = RG[0].astype(F32)
    for i in range(1, 8):
        g = g + RG[i].astype(F32)
    G32[...] = g
    outs.append(localcopy(G32, o_g))
    wc.wait_recv()
    outs.append(localcopy(WG, o_wg))
    GG[x, zl, c] = g.astype(BF16)
    ga = [remote(GG.at[x, zl, c], GG.at[x, zl, c], dev(dzl=i)) for i in range(1, 4)]

    for r in zs:
        r.wait_recv()
    pj = RZ[0]
    for i in range(1, 8):
        pj = pj + RZ[i]
    for r in ga:
        r.wait_recv()
    gr = remote(GG.at[x, :, c], GG.at[x, :, c], dev(dx=1))
    gl = remote(GG.at[x, :, c], GG.at[x, :, c], dev(dx=3))
    gcs = [remote(GG.at[x, :, c], GG.at[x, :, c], dev(core=oc))]
    for r in ld_m:
        r.wait()
    ycol = pl.ds(pl.multiple_of(y * 128, 128), 128)
    first = 0.9 * MI[0, :, ycol] + 0.1 * pj
    second = 0.999 * MI[1, :, ycol] + 0.001 * pj * pj
    tilde = first / BIAS1 / (jnp.sqrt(second / BIAS2) + 1e-08)
    raw = jnp.sum(pj * pj, 0, keepdims=True)
    til = jnp.sum(tilde * tilde, 0, keepdims=True)
    r8 = lax.broadcasted_iota(jnp.int32, (8, 128), 0)
    VS[zl, c] = jnp.where(r8 == 0, raw, jnp.where(r8 == 1, til, 0.0))
    vs = [remote(VS.at[zl, c], VS.at[zl, c], dev(dzl=i, core=cc))
          for i, cc in ((2, c), (2, oc), (1, c), (3, c), (1, oc), (3, oc), (0, oc))]
    MO[y, 0] = first
    MO[y, 1] = second
    mo = [remote(MO.at[y], MO.at[y], dev(dy=i)) for i in range(1, 4)]
    for r in vs:
        r.wait_recv()
    v = VS[0, 0]
    for i in range(1, 8):
        v = v + VS[i // 2, i % 2]
    VX[x, y] = v
    vx = [remote(VX.at[x, y], VX.at[x, y], dev(dx=i, dy=j))
          for i, j in ((2, 2), (1, 2), (3, 2), (2, 1), (2, 3), (0, 2), (2, 0), (1, 1), (1, 3), (3, 1),
                       (3, 3), (0, 1), (0, 3), (1, 0), (3, 0))]
    for r in mo:
        r.wait_recv()
    outs.append(localcopy(MO, o_mo))
    xl, xr = lax.rem(x + 3, 4), lax.rem(x + 1, 4)
    lo, hi_ = pl.ds(0, 2), pl.ds(2, 2)
    gr.wait_recv()
    fr = remote(GG.at[xl, lo, c], GG.at[xl, lo, c], dev(dx=1))
    gcs.append(remote(GG.at[xl, :, c], GG.at[xl, :, c], dev(core=oc)))
    gl.wait_recv()
    fl = remote(GG.at[xr, hi_, c], GG.at[xr, hi_, c], dev(dx=3))
    gcs.append(remote(GG.at[xr, :, c], GG.at[xr, :, c], dev(core=oc)))
    for r in vx:
        r.wait_recv()
    for j in range(4):
        t = VX[0, j] + VX[1, j] + VX[2, j] + VX[3, j]
        col = 8.0 * (jnp.sqrt(t[1:2]) / jnp.sqrt(t[0:1] + 1e-06))
        CS[:, pl.ds(128 * j, 128)] = jnp.broadcast_to(col, (8, 128))
    outs.append(localcopy(CS, o_cs))
    xo = lax.rem(x + 2, 4)
    fr.wait_recv()
    gcs.append(remote(GG.at[xo, lo, c], GG.at[xo, lo, c], dev(core=oc)))
    fl.wait_recv()
    gcs.append(remote(GG.at[xo, hi_, c], GG.at[xo, hi_, c], dev(core=oc)))
    for i, r in ((x, gcs[0]), (xl, gcs[1]), (xr, gcs[2])):
        r.wait_recv()
        outs.append(localcopy(GG.at[i], o_gg.at[i]))
    gcs[3].wait_recv()
    gcs[4].wait_recv()
    outs.append(localcopy(GG.at[xo], o_gg.at[xo]))
    for r in outs:
        r.wait()
    for r in copies:
        r.wait_send()


STEPS = 2
ROWS = 1024 // STEPS


def finish(wg, gg, g32, cs, mo, w32, o_qv, o_qs, o_nw, o_m1, o_m2):
    @pl.when(pl.program_id(0) == 0)
    def _():
        for j in range(4):
            cols = pl.ds(128 * j, 128)
            o_nw[:, cols] = w32[:, cols] - g32[:, cols] * cs[0:1, cols]
            o_m1[:, cols] = mo[j, 0]
            o_m2[:, cols] = mo[j, 1]

    eye = (lax.broadcasted_iota(jnp.int32, (8, 128), 0)
           == lax.broadcasted_iota(jnp.int32, (8, 128), 1)).astype(BF16)
    lane = lax.broadcasted_iota(jnp.int32, (128, 128), 1)
    for i in range(ROWS // 128):
        rows = pl.ds(i * 128, 128)
        packed = jnp.zeros((128, 128), F32)
        for j in range(4):
            cols = pl.ds(128 * j, 128)
            v = wg[rows, cols].astype(F32) - gg[rows, cols].astype(F32) * cs[0:1, cols]
            scale = (jnp.max(jnp.abs(v), 1, keepdims=True) + 1e-06).astype(BF16).astype(F32)
            o_qv[rows, cols] = (v * (1.0 / scale)).astype(BF16)
            packed = jnp.where(lane == j, scale, packed)
        tr = lax.dot_general(eye, packed.astype(BF16), (((1,), (1,)), ((), ())),
                             preferred_element_type=F32)
        o_qs[:, rows] = tr[:4].astype(BF16)


def shards(grad_values, grad_exponents, proj, weights, moment1, moment2):
    gv = grad_values.reshape(8, 4, 4, 2, 32, 512)
    ex = grad_exponents.reshape(4, 8192)
    any_ = pl.BlockSpec(memory_space=pl.ANY)
    V = pltpu.VMEM
    scratch = [
        V((2, 4, 2, 4, 4, 16, 512), BF16),
        V((2, 4, 2, 4, 4, 16, 512), BF16),
        V((2, 4, 2, 4, 4, 16, 512), BF16),
        V((2, 2, 4, 4, 16, 512), BF16),
        V((2, 2, 2, 4, 4, 16, 512), BF16),
        V((2, 4, 2, 4, 16, 512), BF16),
        V((2, 2, 4, 16, 512), BF16),
        V((2, 2, 2, 4, 16, 512), BF16),
        V((8, 32, 512), BF16),
        V((8, 32, 512), BF16),
        V((8, 32, 256), F32),
        V((3, 256, 256), BF16),
        V((4, 4, 2, 8, 512), F32),
        V((4, 4, 8, 512), F32),
        V((4, 4, 32, 128), BF16),
        V((4, 4, 32, 128), BF16),
        V((4, 8, 128), F32),
        V((8, 8, 128), F32),
        V((4, 2, 8, 128), F32),
        V((4, 2, 8, 128), F32),
        V((4, 4, 8, 128), F32),
        V((32, 512), F32),
        V((4, 4, 2, 32, 512), BF16),
        V((4, 4, 2, 32, 512), BF16),
        V((32, 512), F32),
        V((4, 8192), jnp.int32),
        V((4, 8192), jnp.int32),
        V((2, 8, 512), F32),
        V((8, 512), F32),
        V((128, 128), BF16),
        pltpu.SemaphoreType.DMA((NCOPY,)),
        pltpu.SemaphoreType.DMA((NCOPY,)),
        pltpu.SemaphoreType.DMA((40,)),
    ]
    wg, gg, g32, cs, mo = pl.pallas_call(
        kernel,
        out_shape=(
            jax.ShapeDtypeStruct((4, 4, 2, 32, 512), BF16),
            jax.ShapeDtypeStruct((4, 4, 2, 32, 512), BF16),
            jax.ShapeDtypeStruct((32, 512), F32),
            jax.ShapeDtypeStruct((8, 512), F32),
            jax.ShapeDtypeStruct((4, 2, 8, 128), F32),
        ),
        in_specs=[any_] * 6,
        out_specs=(any_,) * 5,
        scratch_shapes=scratch,
        compiler_params=pltpu.CompilerParams(
            collective_id=0, has_side_effects=True, vmem_limit_bytes=60 * 1024 * 1024
        ),
    )(gv, ex, proj, weights, moment1, moment2)
    whole = lambda *shape: pl.BlockSpec(shape, lambda i: (0,) * len(shape))
    return pl.pallas_call(
        finish,
        grid=(STEPS,),
        out_shape=(
            jax.ShapeDtypeStruct((1024, 512), BF16),
            jax.ShapeDtypeStruct((4, 1024), BF16),
            jax.ShapeDtypeStruct((32, 512), F32),
            jax.ShapeDtypeStruct((8, 512), F32),
            jax.ShapeDtypeStruct((8, 512), F32),
        ),
        in_specs=[
            pl.BlockSpec((ROWS, 512), lambda i: (i, 0)),
            pl.BlockSpec((ROWS, 512), lambda i: (i, 0)),
            whole(32, 512), whole(8, 512), whole(4, 2, 8, 128), whole(32, 512),
        ],
        out_specs=(
            pl.BlockSpec((ROWS, 512), lambda i: (i, 0)),
            pl.BlockSpec((4, ROWS), lambda i: (0, i)),
            whole(32, 512), whole(8, 512), whole(8, 512),
        ),
    )(wg.reshape(1024, 512), gg.reshape(1024, 512), g32, cs, mo, weights)


def solution(mesh):
    return jax.shard_map(
        shards,
        mesh=mesh,
        in_specs=(
            P(("node", "local"), None, None),
            P(("node", "local"), None, None),
            P(("local", "node"), None),
            P(("local", "node"), None),
            P("node", None),
            P("node", None),
        ),
        out_specs=(
            P("local", None),
            P(None, "local"),
            P(("local", "node"), None),
            P("node", None),
            P("node", None),
        ),
        check_vma=False,
    )
```

```python
import functools

import jax
import jax.numpy as jnp
from jax import lax
from jax.experimental import pallas as pl
from jax.experimental.pallas import tpu as pltpu
from jax.sharding import PartitionSpec as P

MESH = pl.DeviceIdType.MESH
BIAS1 = 1.0 - 0.9**10
BIAS2 = 1.0 - 0.999**10
F32 = jnp.float32
BF16 = jnp.bfloat16
NCOPY = 160
PRE = 16


def kernel(
    gv, ex, proj, wts, mom1, mom2,
    o_wg, o_gg, o_g, o_cs, o_mo,
    M0, M1, S, RA, RB, S2, RA2, RB2, G2, RG, PA, PT, PP, RP, TQ, RQ, AZ, RZ,
    MO, VS, VX, W32, WG, GG, G32, E0, E1, MI, CS, ONE,
    ss, rs, ls,
):
    node = lax.axis_index("node")
    local = lax.axis_index("local")
    x = lax.div(node, 8)
    zl = lax.rem(lax.div(node, 2), 4)
    c = lax.rem(node, 2)
    zh = lax.div(local, 4)
    y = lax.rem(local, 4)
    z = zh * 4 + zl
    oc = 1 - c

    def dev(dx=0, dy=0, dz=0, core=None, dzl=None):
        xx = lax.rem(x + dx, 4)
        yy = lax.rem(y + dy, 4)
        if dzl is None:
            zz = lax.rem(z + dz, 8)
        else:
            zz = zh * 4 + lax.rem(zl + dzl, 4)
        cc = c if core is None else core
        return (xx * 8 + lax.rem(zz, 4) * 2 + cc, lax.div(zz, 4) * 4 + yy)

    counter = [0]
    copies = []

    def remote(src, dst, to):
        i = counter[0]
        counter[0] += 1
        r = pltpu.make_async_remote_copy(
            src_ref=src, dst_ref=dst, send_sem=ss.at[i], recv_sem=rs.at[i],
            device_id=to, device_id_type=MESH)
        r.start()
        copies.append(r)
        return r

    lcount = [0]

    def localcopy(src, dst):
        i = lcount[0]
        lcount[0] += 1
        r = pltpu.make_async_copy(src, dst, ls.at[i])
        r.start()
        return r

    partners = [dev(core=oc)]
    partners += [dev(dx=i, dy=j) for i in range(4) for j in range(4) if (i, j) != (0, 0)]
    partners += [dev(dz=k) for k in range(1, 8)]
    partners += [dev(dzl=k, core=oc) for k in range(1, 4)]
    barrier = pltpu.get_barrier_semaphore()
    for d in partners:
        pl.semaphore_signal(barrier, inc=1, device_id=d, device_id_type=MESH)

    REL = (2, 1, 3, 0)
    ORDER = ((0, 0), (0, 1), (1, 1), (2, 0), (1, 0), (2, 1), (3, 0), (3, 1))

    def dest(k, di):
        return lax.rem((x if k == 0 else y) + REL[di], 4)

    def gslice(k, di, h, core):
        d = dest(k, di)
        rows = pl.ds(16 * k, 16)
        if k == 0:
            return gv.at[pl.ds(h * 4, 4), d, :, core, rows, :]
        return gv.at[h * 4 + d, :, :, core, rows, :]

    ld_e = localcopy(ex, E0)
    loads = {}
    for di, h in ORDER:
        for k in range(2):
            loads[k, di, h] = localcopy(gslice(k, di, h, c), M0.at[k, di, h])
    ld_w = localcopy(wts, W32)
    ld_p = localcopy(proj, PA.at[z])
    ld_m = [localcopy(mom1, MI.at[0]), localcopy(mom2, MI.at[1])]
    ONE[...] = jnp.ones((128, 128), BF16)

    lane = lax.broadcasted_iota(jnp.int32, (32, 128), 1)
    row = lax.broadcasted_iota(jnp.int32, (32, 128), 0)
    hit0 = row + jnp.where(row >= 16, 48, 0) + c * 32
    masks = [lane == hit0, lane == hit0 + 16]

    def factors(E, k, di, h, q):
        d = dest(k, di)
        rows = []
        for u in range(2):
            for t in range(2):
                base = (((h * 4 + q + u) * 4 + d) if k == 0 else ((h * 4 + d) * 4 + q + u)) * 256 + t * 128
                e = E[:, pl.ds(pl.multiple_of(base, 128), 128)]
                f = 0.5 * lax.shift_left(jnp.ones_like(e), e + 1).astype(F32)
                rows += [jnp.where(masks[k], f[b:b + 1, :], 0.0).astype(BF16) for b in range(4)]
        return jnp.dot(jnp.concatenate(rows, 0), ONE[...], preferred_element_type=F32).astype(BF16)

    def dequant(k, di, h, E, M, add):
        def body(p, carry):
            q = p * 2
            fac = factors(E, k, di, h, q)
            for u in range(2):
                for t in range(2):
                    for b in range(4):
                        for zz in range(2):
                            cols = pl.ds(b * 128, 128)
                            r0 = (((u * 2 + t) * 4 + b) * 2 + zz) * 16
                            v = M[k, di, h, q + u, 2 * t + zz, :, cols] * fac[r0:r0 + 16]
                            if add:
                                v = S[k, di, h, q + u, 2 * t + zz, :, cols] + v
                            S[k, di, h, q + u, 2 * t + zz, :, cols] = v
            return carry

        lax.fori_loop(0, 2, body, 0)

    ld_w.wait()
    WG[x, zl, c] = W32[...].astype(BF16)
    ld_e.wait()
    UNITS = [(k, di, h) for di, h in ORDER for k in range(2)]
    for n, (k, di, h) in enumerate(UNITS):
        if n == PRE:
            break
        loads[k, di, h].wait()
        dequant(k, di, h, E0, M0, False)

    pl.semaphore_wait(barrier, len(partners))

    sendE = remote(ex, E1, dev(core=oc))
    wx = [remote(WG.at[x, zl, c], WG.at[x, zl, c], dev(dx=i)) for i in range(1, 4)]
    sends = {}
    for di, h in ORDER:
        for k in range(2):
            sends[k, di, h] = remote(gslice(k, di, h, oc), M1.at[k, di, h], dev(core=oc))
    pas = [remote(proj, PA.at[z], dev(dz=k)) for k in range(1, 8)]

    def nb(k, stage, step):
        if (k + stage) % 2 == 0:
            return dev(dx=step)
        return dev(dy=step)

    for k, di, h in UNITS[PRE:]:
        loads[k, di, h].wait()
        dequant(k, di, h, E0, M0, False)
    sendE.wait_recv()
    RAc, RBc = {}, {}

    def addinto(dst, src):
        def body(i, carry):
            q, r = lax.div(i, 4), lax.rem(i, 4)
            dst[q, r] = dst[q, r] + src[q, r]
            return carry
        lax.fori_loop(0, 16, body, 0, unroll=4)

    for n, (di, h) in enumerate(ORDER):
        for k in range(2):
            sends[k, di, h].wait_recv()
            dequant(k, di, h, E1, M1, True)
            step = 1 if h == 0 else 3
            if di == 0:
                RAc[k, h] = remote(S.at[k, 0, h], RA.at[k, h], nb(k, 0, step))
            elif (di, h) == (1, 1):
                RBc[k, 0, 1] = remote(S.at[k, 1, 1], RB.at[k, 0, 1], nb(k, 0, 1))
            elif (di, h) == (2, 0):
                RBc[k, 1, 0] = remote(S.at[k, 2, 0], RB.at[k, 1, 0], nb(k, 0, 3))
        if n == 3:
            for r in wx:
                r.wait_recv()
            wz = [remote(WG.at[:, zl, c], WG.at[:, zl, c], dev(dzl=i)) for i in range(1, 4)]
    for h in range(2):
        for k in range(2):
            RAc[k, h].wait_recv()
            di = 1 if h == 0 else 2
            addinto(S.at[k, di, h], RA.at[k, h])
            if h == 0:
                RBc[k, 0, 0] = remote(S.at[k, 1, 0], RB.at[k, 0, 0], nb(k, 0, 1))
            else:
                RBc[k, 1, 1] = remote(S.at[k, 2, 1], RB.at[k, 1, 1], nb(k, 0, 3))


    ld_p.wait()
    for r in pas:
        r.wait_recv()
    pt = jnp.transpose(PA[...].reshape(256, 256))
    hi = pt.astype(BF16)
    rest = pt - hi.astype(F32)
    mid = rest.astype(BF16)
    PT[0] = hi
    PT[1] = mid
    PT[2] = (rest - mid.astype(F32)).astype(BF16)

    RAc2, RBc2 = {}, {}

    def finish1(k, di, h):
        a = lax.rem((y if k == 0 else x) + REL[di], 4)
        for r in range(4):
            v = (S[k, 3, h, a, r].astype(F32) + RB[k, 0, h, a, r].astype(F32)
                 + RB[k, 1, h, a, r].astype(F32))
            S2[k, di, h, r] = v.astype(BF16)

    for k in range(2):
        for s in range(2):
            for h in ((1, 0) if s == 0 else (0, 1)):
                RBc[k, s, h].wait_recv()
    for di, h in ORDER:
        for k in range(2):
            finish1(k, di, h)
            step = 1 if h == 0 else 3
            if di == 0:
                RAc2[k, h] = remote(S2.at[k, 0, h], RA2.at[k, h], nb(k, 1, step))
            elif (di, h) == (1, 1):
                RBc2[k, 0, 1] = remote(S2.at[k, 1, 1], RB2.at[k, 0, 1], nb(k, 1, 1))
            elif (di, h) == (2, 0):
                RBc2[k, 1, 0] = remote(S2.at[k, 2, 0], RB2.at[k, 1, 0], nb(k, 1, 3))
    for h in range(2):
        for k in range(2):
            RAc2[k, h].wait_recv()
            di = 1 if h == 0 else 2
            for r in range(4):
                S2[k, di, h, r] = S2[k, di, h, r] + RA2[k, h, r]
            if h == 0:
                RBc2[k, 0, 0] = remote(S2.at[k, 1, 0], RB2.at[k, 0, 0], nb(k, 1, 1))
            else:
                RBc2[k, 1, 1] = remote(S2.at[k, 2, 1], RB2.at[k, 1, 1], nb(k, 1, 3))
    for k in range(2):
        for s in range(2):
            for h in ((1, 0) if s == 0 else (0, 1)):
                RBc2[k, s, h].wait_recv()
        for h in range(2):
            for r in range(4):
                v = (S2[k, 3, h, r].astype(F32) + RB2[k, 0, h, r].astype(F32)
                     + RB2[k, 1, h, r].astype(F32))
                G2[h * 4 + r, pl.ds(16 * k, 16), :] = v.astype(BF16)

    gz = [remote(G2.at[lax.rem(z + k, 8)], RG.at[z], dev(dz=k)) for k in (4, 3, 5, 2, 6, 1, 7)]

    g2 = G2[...].reshape(256, 512)
    part = (jnp.dot(PT[0], g2, preferred_element_type=F32)
            + jnp.dot(PT[1], g2, preferred_element_type=F32)
            + jnp.dot(PT[2], g2, preferred_element_type=F32))
    PP[...] = part.reshape(4, 4, 2, 8, 512)
    pc = remote(PP.at[:, :, oc], RP, dev(core=oc))
    pc.wait_recv()
    for i in range(4):
        for r in range(4):
            v = PP[i, r, c] + RP[i, r]
            for j in range(4):
                TQ[i, j, pl.ds(8 * r, 8), :] = v[:, j * 128:(j + 1) * 128].astype(BF16)
    RQ[x, y] = TQ[x, y]
    qs = [remote(TQ.at[lax.rem(x + i, 4), lax.rem(y + j, 4)], RQ.at[x, y], dev(dx=i, dy=j))
          for i in range(4) for j in range(4) if (i, j) != (0, 0)]
    for r in qs:
        r.wait_recv()
    acc = RQ[0, 0].astype(F32)
    for i in range(1, 16):
        acc = acc + RQ[i // 4, i % 4].astype(F32)
    AZ[...] = acc.reshape(4, 8, 128)
    RZ[z] = AZ[zl]
    zs = [remote(AZ.at[lax.rem(zl + k, 4)], RZ.at[z], dev(dz=k)) for k in range(1, 8)]

    for r in wz:
        r.wait_recv()
    wc = remote(WG.at[:, :, c], WG.at[:, :, c], dev(core=oc))
    outs = []

    for r in gz:
        r.wait_recv()
    RG[z] = G2[z]
    g = RG[0].astype(F32)
    for i in range(1, 8):
        g = g + RG[i].astype(F32)
    G32[...] = g
    outs.append(localcopy(G32, o_g))
    wc.wait_recv()
    outs.append(localcopy(WG, o_wg))
    GG[x, zl, c] = g.astype(BF16)
    ga = [remote(GG.at[x, zl, c], GG.at[x, zl, c], dev(dzl=i)) for i in range(1, 4)]

    for r in zs:
        r.wait_recv()
    pj = RZ[0]
    for i in range(1, 8):
        pj = pj + RZ[i]
    for r in ga:
        r.wait_recv()
    gr = remote(GG.at[x, :, c], GG.at[x, :, c], dev(dx=1))
    gl = remote(GG.at[x, :, c], GG.at[x, :, c], dev(dx=3))
    gcs = [remote(GG.at[x, :, c], GG.at[x, :, c], dev(core=oc))]
    for r in ld_m:
        r.wait()
    ycol = pl.ds(pl.multiple_of(y * 128, 128), 128)
    first = 0.9 * MI[0, :, ycol] + 0.1 * pj
    second = 0.999 * MI[1, :, ycol] + 0.001 * pj * pj
    tilde = first / BIAS1 / (jnp.sqrt(second / BIAS2) + 1e-08)
    raw = jnp.sum(pj * pj, 0, keepdims=True)
    til = jnp.sum(tilde * tilde, 0, keepdims=True)
    r8 = lax.broadcasted_iota(jnp.int32, (8, 128), 0)
    VS[zl, c] = jnp.where(r8 == 0, raw, jnp.where(r8 == 1, til, 0.0))
    vs = [remote(VS.at[zl, c], VS.at[zl, c], dev(dzl=i, core=cc))
          for i, cc in ((2, c), (2, oc), (1, c), (3, c), (1, oc), (3, oc), (0, oc))]
    MO[y, 0] = first
    MO[y, 1] = second
    mo = [remote(MO.at[y], MO.at[y], dev(dy=i)) for i in range(1, 4)]
    for r in vs:
        r.wait_recv()
    v = VS[0, 0]
    for i in range(1, 8):
        v = v + VS[i // 2, i % 2]
    VX[x, y] = v
    vx = [remote(VX.at[x, y], VX.at[x, y], dev(dx=i, dy=j))
          for i, j in ((2, 2), (1, 2), (3, 2), (2, 1), (2, 3), (0, 2), (2, 0), (1, 1), (1, 3), (3, 1),
                       (3, 3), (0, 1), (0, 3), (1, 0), (3, 0))]
    for r in mo:
        r.wait_recv()
    outs.append(localcopy(MO, o_mo))
    xl, xr = lax.rem(x + 3, 4), lax.rem(x + 1, 4)
    lo, hi_ = pl.ds(0, 2), pl.ds(2, 2)
    gr.wait_recv()
    fr = remote(GG.at[xl, lo, c], GG.at[xl, lo, c], dev(dx=1))
    gcs.append(remote(GG.at[xl, :, c], GG.at[xl, :, c], dev(core=oc)))
    gl.wait_recv()
    fl = remote(GG.at[xr, hi_, c], GG.at[xr, hi_, c], dev(dx=3))
    gcs.append(remote(GG.at[xr, :, c], GG.at[xr, :, c], dev(core=oc)))
    for r in vx:
        r.wait_recv()
    for j in range(4):
        t = VX[0, j] + VX[1, j] + VX[2, j] + VX[3, j]
        col = 8.0 * (jnp.sqrt(t[1:2]) / jnp.sqrt(t[0:1] + 1e-06))
        CS[:, pl.ds(128 * j, 128)] = jnp.broadcast_to(col, (8, 128))
    outs.append(localcopy(CS, o_cs))
    xo = lax.rem(x + 2, 4)
    fr.wait_recv()
    gcs.append(remote(GG.at[xo, lo, c], GG.at[xo, lo, c], dev(core=oc)))
    fl.wait_recv()
    gcs.append(remote(GG.at[xo, hi_, c], GG.at[xo, hi_, c], dev(core=oc)))
    for i, r in ((x, gcs[0]), (xl, gcs[1]), (xr, gcs[2])):
        r.wait_recv()
        outs.append(localcopy(GG.at[i], o_gg.at[i]))
    gcs[3].wait_recv()
    gcs[4].wait_recv()
    outs.append(localcopy(GG.at[xo], o_gg.at[xo]))
    for r in outs:
        r.wait()
    for r in copies:
        r.wait_send()


STEPS = 2
ROWS = 1024 // STEPS


def finish(wg, gg, g32, cs, mo, w32, o_qv, o_qs, o_nw, o_m1, o_m2):
    @pl.when(pl.program_id(0) == 0)
    def _():
        for j in range(4):
            cols = pl.ds(128 * j, 128)
            o_nw[:, cols] = w32[:, cols] - g32[:, cols] * cs[0:1, cols]
            o_m1[:, cols] = mo[j, 0]
            o_m2[:, cols] = mo[j, 1]

    eye = (lax.broadcasted_iota(jnp.int32, (8, 128), 0)
           == lax.broadcasted_iota(jnp.int32, (8, 128), 1)).astype(BF16)
    lane = lax.broadcasted_iota(jnp.int32, (128, 128), 1)
    for i in range(ROWS // 128):
        rows = pl.ds(i * 128, 128)
        packed = jnp.zeros((128, 128), F32)
        for j in range(4):
            cols = pl.ds(128 * j, 128)
            v = wg[rows, cols].astype(F32) - gg[rows, cols].astype(F32) * cs[0:1, cols]
            scale = (jnp.max(jnp.abs(v), 1, keepdims=True) + 1e-06).astype(BF16).astype(F32)
            o_qv[rows, cols] = (v * (1.0 / scale)).astype(BF16)
            packed = jnp.where(lane == j, scale, packed)
        tr = lax.dot_general(eye, packed.astype(BF16), (((1,), (1,)), ((), ())),
                             preferred_element_type=F32)
        o_qs[:, rows] = tr[:4].astype(BF16)


def shards(grad_values, grad_exponents, proj, weights, moment1, moment2):
    gv = grad_values.reshape(8, 4, 4, 2, 32, 512)
    ex = grad_exponents.reshape(4, 8192)
    any_ = pl.BlockSpec(memory_space=pl.ANY)
    V = pltpu.VMEM
    scratch = [
        V((2, 4, 2, 4, 4, 16, 512), BF16),
        V((2, 4, 2, 4, 4, 16, 512), BF16),
        V((2, 4, 2, 4, 4, 16, 512), BF16),
        V((2, 2, 4, 4, 16, 512), BF16),
        V((2, 2, 2, 4, 4, 16, 512), BF16),
        V((2, 4, 2, 4, 16, 512), BF16),
        V((2, 2, 4, 16, 512), BF16),
        V((2, 2, 2, 4, 16, 512), BF16),
        V((8, 32, 512), BF16),
        V((8, 32, 512), BF16),
        V((8, 32, 256), F32),
        V((3, 256, 256), BF16),
        V((4, 4, 2, 8, 512), F32),
        V((4, 4, 8, 512), F32),
        V((4, 4, 32, 128), BF16),
        V((4, 4, 32, 128), BF16),
        V((4, 8, 128), F32),
        V((8, 8, 128), F32),
        V((4, 2, 8, 128), F32),
        V((4, 2, 8, 128), F32),
        V((4, 4, 8, 128), F32),
        V((32, 512), F32),
        V((4, 4, 2, 32, 512), BF16),
        V((4, 4, 2, 32, 512), BF16),
        V((32, 512), F32),
        V((4, 8192), jnp.int32),
        V((4, 8192), jnp.int32),
        V((2, 8, 512), F32),
        V((8, 512), F32),
        V((128, 128), BF16),
        pltpu.SemaphoreType.DMA((NCOPY,)),
        pltpu.SemaphoreType.DMA((NCOPY,)),
        pltpu.SemaphoreType.DMA((40,)),
    ]
    wg, gg, g32, cs, mo = pl.pallas_call(
        kernel,
        out_shape=(
            jax.ShapeDtypeStruct((4, 4, 2, 32, 512), BF16),
            jax.ShapeDtypeStruct((4, 4, 2, 32, 512), BF16),
            jax.ShapeDtypeStruct((32, 512), F32),
            jax.ShapeDtypeStruct((8, 512), F32),
            jax.ShapeDtypeStruct((4, 2, 8, 128), F32),
        ),
        in_specs=[any_] * 6,
        out_specs=(any_,) * 5,
        scratch_shapes=scratch,
        compiler_params=pltpu.CompilerParams(
            collective_id=0, has_side_effects=True, vmem_limit_bytes=60 * 1024 * 1024
        ),
    )(gv, ex, proj, weights, moment1, moment2)
    whole = lambda *shape: pl.BlockSpec(shape, lambda i: (0,) * len(shape))
    return pl.pallas_call(
        finish,
        grid=(STEPS,),
        out_shape=(
            jax.ShapeDtypeStruct((1024, 512), BF16),
            jax.ShapeDtypeStruct((4, 1024), BF16),
            jax.ShapeDtypeStruct((32, 512), F32),
            jax.ShapeDtypeStruct((8, 512), F32),
            jax.ShapeDtypeStruct((8, 512), F32),
        ),
        in_specs=[
            pl.BlockSpec((ROWS, 512), lambda i: (i, 0)),
            pl.BlockSpec((ROWS, 512), lambda i: (i, 0)),
            whole(32, 512), whole(8, 512), whole(4, 2, 8, 128), whole(32, 512),
        ],
        out_specs=(
            pl.BlockSpec((ROWS, 512), lambda i: (i, 0)),
            pl.BlockSpec((4, ROWS), lambda i: (0, i)),
            whole(32, 512), whole(8, 512), whole(8, 512),
        ),
    )(wg.reshape(1024, 512), gg.reshape(1024, 512), g32, cs, mo, weights)


def solution(mesh):
    return jax.shard_map(
        shards,
        mesh=mesh,
        in_specs=(
            P(("node", "local"), None, None),
            P(("node", "local"), None, None),
            P(("local", "node"), None),
            P(("local", "node"), None),
            P("node", None),
            P("node", None),
        ),
        out_specs=(
            P("local", None),
            P(None, "local"),
            P(("local", "node"), None),
            P("node", None),
            P("node", None),
        ),
        check_vma=False,
    )
```
